32 devices in a mesh: section: 4 (over z), dp: 8 (over y, x, core).
Axes of the slice: x: 2, y: 2, z: 4, core: 2. Of those that a mesh axis runs over, the one named last changes fastest.
Arguments:
- patches: bfloat16 [8192, 1280], P('dp'), may hold values from -6 to 6
- pre_gain: float32 [1280], replicated, may hold values from 0.1 to 1.9
- merge_gain: float32 [1280], replicated, may hold values from 0.1 to 1.9
- merge_bias: float32 [1280], replicated, may hold values from -3 to 3
- w_in: bfloat16 [1280, 2560], P('dp', 'section'), may hold values from -0.15625 to 0.15625
- w_out: bfloat16 [2560, 1280], P('section', 'dp'), may hold values from -0.125 to 0.125
- destinations: int32 [2048, 1], P(('section', 'dp')), may hold values from 0 to 7; in each aligned block of 64 rows (0 to 63, 64 to 127, ...) at most 8 rows name the same one
- upstream: bfloat16 [2048, 5120], P(('section', 'dp')), may hold values from -6 to 6
Outputs:
- received: bfloat16 [2048, 5120], P(('section', 'dp'))
- grad_w_in: float32 [1280, 2560], P('dp', 'section')
- grad_w_out: float32 [2560, 1280], P('section', 'dp')
The draws below stay inside these ranges and needn't reach their ends.
Inputs may be any that keep to these rules, and one draw needn't show every extreme that they name: `destinations`: among the 64 blocks of one device, one replica is named at most 8 times, and exactly 8 times for some replica in some devices.
All inputs are finite; a program needn't handle non-finite values.
Results may differ from the reference program's by a relative error of at most 0.0068.
Values may be sent and summed in bfloat16 or wider, within the bound.
A program may use at most 128 MiB of HBM per device.

```python
import math
import jax
import jax.numpy as jnp
import numpy as np
from jax import lax

DV = 1280
FFW = 2560
MERGE = 4
BLK = 1
NBLK = 64
DM = 5120
CAP = 8
PATCH_GROUP = 1024
PATCHES = 8192
SLOTS = 64
N_SECTION = 4
N_DP = 8


def strengthened(values, own_key, source, target, parts, factor):
    owner, partner = [(jnp.arange(values.shape[dim]) // (values.shape[dim] // parts)).reshape([-1 if axis == dim else 1 for axis in range(values.ndim)]) for dim in (source, target)]
    chosen = jax.random.permutation(own_key, parts)[partner]
    strong = (owner == chosen) | (owner == (partner + parts // 2) % parts)
    return jnp.where(strong, factor * values, values)


def block_scale(key, dims, pieces, smallest, largest):
    level, own = 1.0, jax.random.fold_in(key, 6)
    for dim, shards_of in pieces:
        draws = jnp.exp(jax.random.uniform(jax.random.fold_in(own, dim), (shards_of,), jnp.float32, smallest / len(pieces), largest / len(pieces)))
        level = level * jnp.repeat(draws, dims[dim] // shards_of).reshape([-1 if axis == dim else 1 for axis in range(len(dims))])
    return level


def routed_block(key, own, number, rows, number_of, top, bound, lean):
    sequence = jax.random.permutation(key, number_of)
    packed, usual = shares(number_of, rows * top, bound, lean, True), shares(number_of, rows * top, bound, lean, False)
    places = jnp.arange(number_of)

    def named(sizes, offset_by):
        used = int((sizes > 0).sum())
        fixed = max(1, used // 4)
        moved = fixed + (places - fixed + offset_by * (used - fixed)) % max(1, number_of - fixed)
        return jnp.zeros((number_of,), jnp.int32).at[sequence[jnp.where(places < fixed, places, moved)]].set(jnp.asarray(sizes, jnp.int32))

    sizes = jnp.where(number % 4 == 0, named(packed, number // 4), named(usual, number - number // 4 - 1))
    mixed = jax.random.permutation(jax.random.fold_in(own, 3), number_of)
    giver, sink = mixed[0:number_of // 2 * 2:2], mixed[1:number_of // 2 * 2:2]
    slack = jnp.minimum(sizes[giver] - 1, bound - sizes[sink]) // 2
    slack = jnp.where((giver == sequence[0]) | (sink == sequence[0]) | (sizes[sink] == 0), 0, jnp.maximum(slack, 0))
    moved = jax.random.randint(jax.random.fold_in(own, 4), (number_of // 2,), 0, 1 << 20) % (slack + 1)
    sizes = sizes.at[giver].add(-moved).at[sink].add(moved)
    labels = jnp.searchsorted(jnp.cumsum(sizes), jnp.arange(rows * top), side="right").astype(jnp.int32)
    grid = labels.reshape(top, rows).T
    grid = grid[jax.random.permutation(jax.random.fold_in(own, 1), rows)]
    offset_by = jax.random.randint(jax.random.fold_in(own, 2), (rows, 1), 0, top)
    return jnp.take_along_axis(grid, (jnp.arange(top)[None, :] + offset_by) % top, axis=1)


def shares(number_of, total, reach, lean, full):
    loads = [(1 << 20) // math.isqrt(rank ** lean) + 1 for rank in range(1, number_of + 1)]
    largest = reach if full else min(reach, max(-(-total // number_of), total * loads[0] // sum(loads)))
    least = 1 if total - largest >= number_of - 1 else 0
    counts, spare = [largest] + [least] * (number_of - 1), total - largest - least * (number_of - 1)
    while spare > 0:
        free = [i for i in range(1, number_of) if counts[i] < largest] or [i for i in range(1, number_of) if counts[i] < reach]
        mass, left = sum([loads[i] for i in free]), spare
        for i in free:
            extra = min(reach - counts[i], max(1, left * loads[i] // mass), spare)
            counts[i] = counts[i] + extra
            spare = spare - extra
    return np.array(counts)


def noise(stream_key, shape, spread, limit, pieces=(), kind=jnp.bfloat16):
    level = block_scale(stream_key, shape, pieces, -0.22, 0.18) if pieces else 1.0
    drawn = jax.random.normal(stream_key, shape, jnp.float32) * spread * level
    return jnp.minimum(jnp.maximum(drawn, -limit), limit).astype(kind)


def heavy_noise(rng, shape, scale, reach, pieces, heavy, held_as=jnp.bfloat16):
    result = scale * jax.random.normal(rng, shape, jnp.float32)
    if pieces:
        result = result * block_scale(rng, shape, pieces, -0.22, 0.18)
    return jnp.clip(strengthened(result, jax.random.fold_in(rng, 3), *heavy), -reach, reach).astype(held_as)


def setup_inputs(seed: int = 0) -> dict:
    key_of = jax.random.split(jax.random.key(seed), 9)
    patches = heavy_noise(key_of[0], (PATCHES, DV), 1.0, 6.0, ((0, 8),), (0, 1, 8, 2.0))
    pre_gain = jnp.clip(1.0 + 0.18 * jax.random.normal(key_of[1], (DV,), jnp.float32), 0.1, 1.9)
    merge_gain = jnp.clip(1.0 + 0.18 * jax.random.normal(key_of[2], (DV,), jnp.float32), 0.1, 1.9)
    merge_bias = noise(key_of[3], (DV,), 0.5, 3.0, (), jnp.float32)
    w_in = noise(key_of[4], (DV, FFW), DV ** -0.5, 0.15625, ((0, 8), (1, 4)))
    w_out = noise(key_of[5], (FFW, DV), FFW ** -0.5, 0.125, ((0, 4), (1, 8)))
    destinations_keys = jax.random.split(jax.random.fold_in(key_of[6], 1), (N_SECTION * N_DP * NBLK) // NBLK)
    destinations_turns = jax.random.permutation(jax.random.fold_in(key_of[6], 3), (N_SECTION * N_DP * NBLK) // NBLK)
    destinations = jax.vmap(lambda own, number: routed_block(jax.random.fold_in(key_of[6], 2), own, number, NBLK, N_DP, 1, CAP, 2))(destinations_keys, destinations_turns).reshape((N_SECTION * N_DP * NBLK, 1))
    upstream = noise(key_of[7], (N_SECTION * N_DP * SLOTS, DM), 1.0, 6.0, ((0, 32),))
    return dict(patches=patches, pre_gain=pre_gain, merge_gain=merge_gain, merge_bias=merge_bias, w_in=w_in, w_out=w_out, destinations=destinations, upstream=upstream)


epsilon = 1e-06
gelu_scale = 0.7978845608028654
gelu_cubic = 0.044715

def gelu_slope(values):
    tangent = jnp.tanh(gelu_scale * (values + gelu_cubic * values * values * values))
    return 0.5 * (1.0 + tangent) + 0.5 * values * (1.0 - tangent * tangent) * gelu_scale * (1.0 + 3.0 * gelu_cubic * values * values)

def normalize(values):
    average = lax.optimization_barrier(jnp.mean(values, axis=-1, keepdims=True))
    centred = values - average
    inv_scale = lax.rsqrt(lax.optimization_barrier(jnp.mean(centred * centred, axis=-1, keepdims=True)) + epsilon)
    return (centred * inv_scale, inv_scale)

def norm_backward(cotangent, unit_rows, inv_scale, gain):
    scaled = cotangent * gain
    return inv_scale * (scaled - lax.optimization_barrier(jnp.mean(scaled, axis=-1, keepdims=True)) - unit_rows * lax.optimization_barrier(jnp.mean(scaled * unit_rows, axis=-1, keepdims=True)))

def block_ranks(targets):
    block_count = targets.shape[-1]
    matches = targets[..., :, None] == targets[..., None, :]
    earlier = lax.broadcasted_iota(jnp.int32, (block_count, block_count), 1) < lax.broadcasted_iota(jnp.int32, (block_count, block_count), 0)
    return lax.optimization_barrier(jnp.sum((matches & earlier).astype(jnp.int32), axis=-1))

def reference(patches, pre_gain, merge_gain, merge_bias, w_in, w_out, destinations, upstream):
    group_rows = PATCH_GROUP
    block_width = BLK * MERGE * DV

    def forward(replica):
        group_x = lax.dynamic_slice_in_dim(patches, (replica * group_rows).astype(jnp.int32), group_rows, 0).astype(jnp.float32)
        unit_rows, _ = normalize(group_x)
        normed = (unit_rows * pre_gain).astype(jnp.bfloat16)
        preact = jnp.dot(normed, w_in, preferred_element_type=jnp.float32)
        hidden = jax.nn.gelu(preact, approximate=True).astype(jnp.bfloat16)
        residual = group_x + jnp.dot(hidden, w_out, preferred_element_type=jnp.float32)
        unit_out, _ = normalize(residual)
        merged = (unit_out * merge_gain + merge_bias).astype(jnp.bfloat16)
        return (normed, preact, residual, merged)
    normed_all, preact_all, residual_all, merged_all = lax.map(forward, jnp.arange(N_DP, dtype=jnp.int32))
    blocks = merged_all.reshape(N_DP, N_SECTION, NBLK, block_width).transpose(1, 0, 2, 3).reshape(N_SECTION * N_DP * NBLK, block_width)
    targets = destinations.reshape(N_SECTION * N_DP, NBLK)
    block_rank = block_ranks(targets)
    device_ids = lax.broadcasted_iota(jnp.int32, (N_SECTION * N_DP, NBLK), 0)
    slot_index = ((device_ids // N_DP * N_DP + targets) * N_DP + device_ids % N_DP) * CAP + block_rank
    slot_index = slot_index.reshape(-1).astype(jnp.int32)
    received = jnp.zeros((N_SECTION * N_DP * N_DP * CAP, block_width), jnp.bfloat16).at[slot_index].set(blocks)
    received = received.reshape(N_SECTION * N_DP * N_DP * CAP * BLK, MERGE * DV)
    back_blocks = upstream.reshape(N_SECTION * N_DP * N_DP * CAP, block_width)[slot_index]
    back_rows = back_blocks.reshape(N_SECTION, N_DP, NBLK, block_width).transpose(1, 0, 2, 3).reshape(N_DP, group_rows, DV)

    def accumulate(totals, sample_item):
        normed, preact, residual, cotangent = sample_item
        unit_rows, inv_scale = normalize(residual)
        grad_residual = norm_backward(cotangent.astype(jnp.float32), unit_rows, inv_scale, merge_gain).astype(jnp.bfloat16)
        grad_hidden = lax.dot_general(grad_residual, w_out, (((1,), (1,)), ((), ())), preferred_element_type=jnp.float32)
        grad_preact = (grad_hidden * gelu_slope(preact)).astype(jnp.bfloat16)
        hidden = jax.nn.gelu(preact, approximate=True).astype(jnp.bfloat16)
        grad_first = totals[0] + lax.dot_general(normed, grad_preact, (((0,), (0,)), ((), ())), preferred_element_type=jnp.float32)
        grad_second = totals[1] + lax.dot_general(hidden, grad_residual, (((0,), (0,)), ((), ())), preferred_element_type=jnp.float32)
        return ((grad_first, grad_second), None)
    start_totals = (jnp.zeros((DV, FFW), jnp.float32), jnp.zeros((FFW, DV), jnp.float32))
    (grad_w_in, grad_w_out), _ = lax.scan(accumulate, start_totals, (normed_all, preact_all, residual_all, back_rows))
    return (received, grad_w_in, grad_w_out)
```

```python
import jax
import jax.numpy as jnp
from jax import lax
from jax.sharding import PartitionSpec as P

BLK = 1


epsilon = 1e-06
gelu_scale = 0.7978845608028654
gelu_cubic = 0.044715


def gelu_slope(values):
    tangent = jnp.tanh(gelu_scale * (values + gelu_cubic * values * values * values))
    return 0.5 * (1.0 + tangent) + 0.5 * values * (1.0 - tangent * tangent) * gelu_scale * (
        1.0 + 3.0 * gelu_cubic * values * values
    )


def normalize(values):
    average = jnp.mean(values, axis=-1, keepdims=True)
    centred = values - average
    inv_scale = lax.rsqrt(jnp.mean(centred * centred, axis=-1, keepdims=True) + epsilon)
    return (centred * inv_scale, inv_scale)


def norm_backward(cotangent, unit_rows, inv_scale, gain):
    scaled = cotangent * gain
    return inv_scale * (
        scaled
        - jnp.mean(scaled, axis=-1, keepdims=True)
        - unit_rows * jnp.mean(scaled * unit_rows, axis=-1, keepdims=True)
    )


def block_ranks(targets):
    block_count = targets.shape[-1]
    matches = targets[:, None] == targets[None, :]
    earlier = lax.broadcasted_iota(jnp.int32, (block_count, block_count), 1) < lax.broadcasted_iota(
        jnp.int32, (block_count, block_count), 0
    )
    return jnp.sum((matches & earlier).astype(jnp.int32), axis=-1)


def on_device(patches, pre_gain, merge_gain, merge_bias, w_in, w_out, destinations, upstream):
    sections = lax.axis_size("section")
    replicas = lax.axis_size("dp")
    group_rows = patches.shape[0]
    share_rows = group_rows // sections
    feature_count = patches.shape[1]
    merged_width = upstream.shape[1]
    block_width = BLK * merged_width
    block_count = destinations.shape[0]
    capacity = upstream.shape[0] // (replicas * BLK)
    inputs = patches.astype(jnp.float32)
    unit_rows, _ = normalize(inputs)
    normed = (unit_rows * pre_gain).astype(jnp.bfloat16)
    preact = jnp.dot(
        normed, lax.all_gather(w_in, "dp", axis=0, tiled=True), preferred_element_type=jnp.float32
    )
    hidden = jax.nn.gelu(preact, approximate=True).astype(jnp.bfloat16)
    out_full = lax.all_gather(w_out, "dp", axis=1, tiled=True)
    partial_value = jnp.dot(hidden, out_full, preferred_element_type=jnp.float32).astype(jnp.bfloat16)
    row_start = lax.axis_index("section") * share_rows
    own_inputs = lax.dynamic_slice_in_dim(inputs, row_start, share_rows, 0)
    residual = own_inputs + lax.psum_scatter(
        partial_value, "section", scatter_dimension=0, tiled=True
    ).astype(jnp.float32)
    unit_out, scale_out = normalize(residual)
    merged = (unit_out * merge_gain + merge_bias).astype(jnp.bfloat16)
    blocks = merged.reshape(block_count, block_width)
    targets = destinations[:, 0]
    block_rank = block_ranks(targets)
    column_ids = lax.broadcasted_iota(jnp.int32, (block_count, replicas * capacity), 1)
    picker = ((targets * capacity + block_rank)[:, None] == column_ids).astype(jnp.bfloat16)
    outgoing = lax.dot_general(
        picker, blocks, (((0,), (0,)), ((), ())), preferred_element_type=jnp.float32
    ).astype(jnp.bfloat16)
    arrived = lax.all_to_all(
        outgoing.reshape(replicas, capacity * block_width),
        "dp",
        split_axis=0,
        concat_axis=0,
        tiled=True,
    )
    received = arrived.reshape(replicas * capacity * BLK, merged_width)
    coming = lax.all_to_all(
        upstream.reshape(replicas, capacity * block_width),
        "dp",
        split_axis=0,
        concat_axis=0,
        tiled=True,
    )
    cotangent = jnp.dot(
        picker, coming.reshape(replicas * capacity, block_width), preferred_element_type=jnp.float32
    )
    cotangent = cotangent.astype(jnp.bfloat16).reshape(share_rows, feature_count)
    grad_own = norm_backward(cotangent.astype(jnp.float32), unit_out, scale_out, merge_gain).astype(
        jnp.bfloat16
    )
    grad_residual = lax.all_gather(grad_own, "section", axis=0, tiled=True)
    grad_second = lax.dot_general(
        hidden, grad_residual, (((0,), (0,)), ((), ())), preferred_element_type=jnp.float32
    )
    grad_hidden = lax.dot_general(
        grad_residual, out_full, (((1,), (1,)), ((), ())), preferred_element_type=jnp.float32
    )
    grad_preact = (grad_hidden * gelu_slope(preact)).astype(jnp.bfloat16)
    grad_first = lax.dot_general(
        normed, grad_preact, (((0,), (0,)), ((), ())), preferred_element_type=jnp.float32
    )
    grad_w_in, grad_w_out = (
        lax.psum_scatter(grad_first.astype(jnp.bfloat16), "dp", scatter_dimension=0, tiled=True).astype(jnp.float32),
        lax.psum_scatter(grad_second.astype(jnp.bfloat16), "dp", scatter_dimension=1, tiled=True).astype(jnp.float32),
    )
    return (received, grad_w_in, grad_w_out)


def solution(mesh):
    return jax.shard_map(
        on_device,
        mesh=mesh,
        in_specs=(
            P("dp", None),
            P(),
            P(),
            P(),
            P("dp", "section"),
            P("section", "dp"),
            P(("section", "dp"), None),
            P(("section", "dp"), None),
        ),
        out_specs=(P(("section", "dp"), None), P("dp", "section"), P("section", "dp")),
        check_vma=False,
    )
```

```python
import functools

import jax
import jax.numpy as jnp
import numpy as np
from jax import lax
from jax.experimental import pallas as pl
from jax.experimental.pallas import tpu as pltpu
from jax.sharding import PartitionSpec as P

BLK = 1


epsilon = 1e-06
gelu_scale = 0.7978845608028654
gelu_cubic = 0.044715


def gelu_slope(values):
    tangent = jnp.tanh(gelu_scale * (values + gelu_cubic * values * values * values))
    return 0.5 * (1.0 + tangent) + 0.5 * values * (1.0 - tangent * tangent) * gelu_scale * (
        1.0 + 3.0 * gelu_cubic * values * values
    )


def normalize(values):
    average = jnp.mean(values, axis=-1, keepdims=True)
    centred = values - average
    inv_scale = lax.rsqrt(jnp.mean(centred * centred, axis=-1, keepdims=True) + epsilon)
    return (centred * inv_scale, inv_scale)


def norm_backward(cotangent, unit_rows, inv_scale, gain):
    scaled = cotangent * gain
    return inv_scale * (
        scaled
        - jnp.mean(scaled, axis=-1, keepdims=True)
        - unit_rows * jnp.mean(scaled * unit_rows, axis=-1, keepdims=True)
    )


def block_ranks(targets):
    block_count = targets.shape[-1]
    matches = targets[:, None] == targets[None, :]
    earlier = lax.broadcasted_iota(jnp.int32, (block_count, block_count), 1) < lax.broadcasted_iota(
        jnp.int32, (block_count, block_count), 0
    )
    return jnp.sum((matches & earlier).astype(jnp.int32), axis=-1)


def on_device(patches, pre_gain, merge_gain, merge_bias, w_in, w_out, destinations, upstream):
    sections = lax.axis_size("section")
    replicas = lax.axis_size("dp")
    group_rows = patches.shape[0]
    share_rows = group_rows // sections
    feature_count = patches.shape[1]
    merged_width = upstream.shape[1]
    block_width = BLK * merged_width
    block_count = destinations.shape[0]
    capacity = upstream.shape[0] // (replicas * BLK)
    inputs = patches.astype(jnp.float32)
    unit_rows, _ = normalize(inputs)
    normed = (unit_rows * pre_gain).astype(jnp.bfloat16)
    preact = jnp.dot(
        normed, lax.all_gather(w_in, "dp", axis=0, tiled=True), preferred_element_type=jnp.float32
    )
    hidden = jax.nn.gelu(preact, approximate=True).astype(jnp.bfloat16)
    out_full = lax.all_gather(w_out, "dp", axis=1, tiled=True)
    partial_value = jnp.dot(hidden, out_full, preferred_element_type=jnp.float32).astype(jnp.bfloat16)
    row_start = lax.axis_index("section") * share_rows
    own_inputs = lax.dynamic_slice_in_dim(inputs, row_start, share_rows, 0)
    residual = own_inputs + lax.psum_scatter(
        partial_value, "section", scatter_dimension=0, tiled=True
    ).astype(jnp.float32)
    unit_out, scale_out = normalize(residual)
    merged = (unit_out * merge_gain + merge_bias).astype(jnp.bfloat16)
    blocks = merged.reshape(block_count, block_width)
    targets = destinations[:, 0]
    block_rank = block_ranks(targets)
    column_ids = lax.broadcasted_iota(jnp.int32, (block_count, replicas * capacity), 1)
    picker = ((targets * capacity + block_rank)[:, None] == column_ids).astype(jnp.bfloat16)
    outgoing = lax.dot_general(
        picker, blocks, (((0,), (0,)), ((), ())), preferred_element_type=jnp.float32
    ).astype(jnp.bfloat16)
    arrived = lax.all_to_all(
        outgoing.reshape(replicas, capacity * block_width),
        "dp",
        split_axis=0,
        concat_axis=0,
        tiled=True,
    )
    received = arrived.reshape(replicas * capacity * BLK, merged_width)
    coming = lax.all_to_all(
        upstream.reshape(replicas, capacity * block_width),
        "dp",
        split_axis=0,
        concat_axis=0,
        tiled=True,
    )
    cotangent = jnp.dot(
        picker, coming.reshape(replicas * capacity, block_width), preferred_element_type=jnp.float32
    )
    cotangent = cotangent.astype(jnp.bfloat16).reshape(share_rows, feature_count)
    grad_own = norm_backward(cotangent.astype(jnp.float32), unit_out, scale_out, merge_gain).astype(
        jnp.bfloat16
    )
    grad_residual = lax.all_gather(grad_own, "section", axis=0, tiled=True)
    grad_second = lax.dot_general(
        hidden, grad_residual, (((0,), (0,)), ((), ())), preferred_element_type=jnp.float32
    )
    grad_hidden = lax.dot_general(
        grad_residual, out_full, (((1,), (1,)), ((), ())), preferred_element_type=jnp.float32
    )
    grad_preact = (grad_hidden * gelu_slope(preact)).astype(jnp.bfloat16)
    grad_first = lax.dot_general(
        normed, grad_preact, (((0,), (0,)), ((), ())), preferred_element_type=jnp.float32
    )
    grad_w_in, grad_w_out = (
        lax.psum_scatter(grad_first.astype(jnp.bfloat16), "dp", scatter_dimension=0, tiled=True).astype(jnp.float32),
        lax.psum_scatter(grad_second.astype(jnp.bfloat16), "dp", scatter_dimension=1, tiled=True).astype(jnp.float32),
    )
    return (received, grad_w_in, grad_w_out)


TILE = 32


def remote(src, dst, send_sem, recv_sem, device):
    return pltpu.make_async_remote_copy(
        src_ref=src,
        dst_ref=dst,
        send_sem=send_sem,
        recv_sem=recv_sem,
        device_id=device,
        device_id_type=pl.DeviceIdType.MESH,
    )


def window_kernel(
    sections, replicas, merge, capacity,
    patches, pre_gain, merge_gain, merge_bias, w_in, w_out_t, tcol, trow, bcol, brow, mcol, mrow, upstream,
    received, grad_in, grad_out,
    rows_in, normed, normed_t, first, second, slope, hidden, part_out, part_in, unit, inv, merged, outgoing,
    coming, cot, grad_rows, grad_rows_t, grad_pre, core_out, core_in, chip_out, chip_in, total, cross_out,
    cross_in, local_sem, gs, gr, us, ur, os_, or_, ps, pr, xs, xr, cs, cr, hs, hr, zs, zr,
):
    share = rows_in.shape[0] // 2
    features = rows_in.shape[1]
    width = w_in.shape[1]
    shard = w_in.shape[0]
    chips = replicas // 2
    f32, bf16 = jnp.float32, jnp.bfloat16
    s, d = lax.axis_index("section"), lax.axis_index("dp")
    q, c = d // 2, d % 2
    pair = (s + 1 - 2 * (s % 2), d)
    across = ((s + sections // 2) % sections, d)
    mate_core = 1 - c
    mate = (s, q * 2 + mate_core)

    def chip_at(k):
        return (q + k) % chips

    def shard_rows(j):
        return pl.ds(pl.multiple_of(j * shard, 16), shard)

    sent = []

    def send(*args):
        copy = remote(*args)
        copy.start()
        sent.append(copy)

    def arrive(dst, recv_sem, send_sem):
        remote(dst, dst, send_sem, recv_sem, mate).wait_recv()

    shards, fulls = (w_in, w_out_t), (first, second)
    loads = [
        pltpu.make_async_copy(
            patches.at[pl.ds(pl.multiple_of(s * share, share), share)], rows_in.at[pl.ds(0, share)], local_sem.at[0]
        ),
        pltpu.make_async_copy(
            patches.at[pl.ds(pl.multiple_of(pair[0] * share, share), share)],
            rows_in.at[pl.ds(share, share)],
            local_sem.at[1],
        ),
        pltpu.make_async_copy(w_in, first.at[0, shard_rows(d)], local_sem.at[2]),
        pltpu.make_async_copy(w_out_t, second.at[0, shard_rows(d)], local_sem.at[3]),
    ]
    slot_rows = capacity * merge
    loads.append(
        pltpu.make_async_copy(
            upstream.at[pl.ds(pl.multiple_of(d * slot_rows, slot_rows), slot_rows)],
            coming.at[pl.ds(pl.multiple_of(d * slot_rows, slot_rows), slot_rows)],
            local_sem.at[4],
        )
    )
    for copy in loads:
        copy.start()

    barrier = pltpu.get_barrier_semaphore()
    for k in range(1, replicas):
        pl.semaphore_signal(
            barrier, inc=1, device_id=(s, (d + k) % replicas), device_id_type=pl.DeviceIdType.MESH
        )
    for peer in (pair, across):
        pl.semaphore_signal(barrier, inc=1, device_id=peer, device_id_type=pl.DeviceIdType.MESH)
    pl.semaphore_wait(barrier, replicas + 1)

    for w in range(2):
        send(shards[w], fulls[w].at[1, shard_rows(d)], gs.at[w, 1, 0], gr.at[w, 1, 0], across)

    def spread(w, b):
        src = shards[w] if b == 0 else fulls[w].at[1, shard_rows(d)]
        for k in range(1, chips):
            send(src, fulls[w].at[b, shard_rows(d)], gs.at[w, b, 1 + k], gr.at[w, b, 1 + k], (s, chip_at(k) * 2 + c))
        send(src, fulls[w].at[b, shard_rows(d)], gs.at[w, b, 1], gr.at[w, b, 1], mate)

    def relay(w, b):
        for k in range(1, chips):
            place = fulls[w].at[b, shard_rows(chip_at(chips - k) * 2 + c)]
            arrive(place, gr.at[w, b, 1 + k], gs.at[w, b, 1 + k])
            send(place, place, gs.at[w, b, chips + k], gr.at[w, b, chips + k], mate)

    def gathered(w, b):
        arrive(fulls[w].at[b, shard_rows(q * 2 + mate_core)], gr.at[w, b, 1], gs.at[w, b, 1])
        for k in range(1, chips):
            place = fulls[w].at[b, shard_rows(chip_at(chips - k) * 2 + mate_core)]
            arrive(place, gr.at[w, b, chips + k], gs.at[w, b, chips + k])

    spread(0, 0)
    arrive(first.at[1, shard_rows(d)], gr.at[0, 1, 0], gs.at[0, 1, 0])
    spread(0, 1)
    spread(1, 0)
    arrive(second.at[1, shard_rows(d)], gr.at[1, 1, 0], gs.at[1, 1, 0])
    spread(1, 1)
    for k in range(1, replicas):
        peer = (d + k) % replicas
        send(
            upstream.at[pl.ds(pl.multiple_of(peer * slot_rows, slot_rows), slot_rows)],
            coming.at[pl.ds(pl.multiple_of(d * slot_rows, slot_rows), slot_rows)],
            us.at[k],
            ur.at[k],
            (s, peer),
        )

    for copy in loads:
        copy.wait()

    def tile_rows(i):
        return pl.ds(pl.multiple_of(i * TILE, TILE), TILE)

    @pl.loop(0, 2 * share // TILE)
    def _(i):
        unit_rows, _ = normalize(rows_in[tile_rows(i), :].astype(f32))
        normed[tile_rows(i), :] = (unit_rows * pre_gain[...]).astype(bf16)

    def flip(src, dst, r):
        @pl.loop(0, features // 128)
        def _(i):
            cols = pl.ds(pl.multiple_of(i * 128, 128), 128)
            dst[cols, pl.ds(r * share, share)] = src[pl.ds(r * share, share), cols].T

    relay(0, 0)
    flip(normed, normed_t, 0)
    flip(normed, normed_t, 1)
    relay(0, 1)

    matches = tcol[...] == trow[...]
    above = jnp.where(matches & (brow[...] < bcol[...]) & (mrow[...] == 0.0), 1.0, 0.0)
    left = jnp.where(matches & (bcol[...] < brow[...]) & (mcol[...] == 0.0), 1.0, 0.0)
    slot_col = (tcol[...] * capacity + jnp.sum(above, axis=1, keepdims=True)) * merge + mcol[...]
    slot_row = (trow[...] * capacity + jnp.sum(left, axis=0, keepdims=True)) * merge + mrow[...]
    lanes = lax.broadcasted_iota(jnp.int32, (share, share), 1).astype(f32)
    subs = lax.broadcasted_iota(jnp.int32, (share, share), 0).astype(f32)

    def half(r):
        return pl.ds(r * share, share)

    for b in range(2):
        gathered(0, b)
        for r in range(2):
            slope[b, half(r), :] = jnp.dot(normed[half(r), :], first[b], preferred_element_type=f32)
        if b == 0:
            relay(1, 0)

        @pl.loop(0, 2 * share // TILE)
        def _(i):
            u = slope[b, tile_rows(i), :]
            tangent = jnp.tanh(gelu_scale * (u + gelu_cubic * u * u * u))
            hidden[b, tile_rows(i), :] = (0.5 * u * (1.0 + tangent)).astype(bf16)
            slope[b, tile_rows(i), :] = 0.5 * (1.0 + tangent) + 0.5 * u * (1.0 - tangent * tangent) * gelu_scale * (
                1.0 + 3.0 * gelu_cubic * u * u
            )

    relay(1, 1)
    gathered(1, 0)
    gathered(1, 1)
    nt = (((1,), (1,)), ((), ()))
    split = features // 2

    def project(r, h):
        value = 0.0
        for b in range(2):
            value = value + lax.dot_general(
                hidden[b, half(r), :], second[b, pl.ds(h * split, split), :], nt, preferred_element_type=f32
            )
        return value

    for h in range(2):
        part_out[h] = project(1, h).astype(bf16)
        send(part_out.at[h], part_in.at[h], ps.at[h], pr.at[h], pair)
    for h in range(2):
        unit[:, pl.ds(h * split, split)] = project(0, h)

    for k in range(1, replicas):
        origin = (d + replicas - k) % replicas
        arrive(
            coming.at[pl.ds(pl.multiple_of(origin * slot_rows, slot_rows), slot_rows)], ur.at[k], us.at[k]
        )
    picker = jnp.where(slot_col == lanes, 1.0, 0.0).astype(bf16)
    cot[...] = jnp.dot(picker, coming[...], preferred_element_type=f32)
    for h in range(2):
        arrive(part_in.at[h], pr.at[h], ps.at[h])

    @pl.loop(0, share // TILE)
    def _(i):
        rows = tile_rows(i)
        partner = jnp.concatenate([part_in[h, rows, :].astype(f32) for h in range(2)], axis=1)
        residual = rows_in[rows, :].astype(f32) + (unit[rows, :] + partner)
        unit_out, scale_out = normalize(residual)
        merged[rows, :] = (unit_out * merge_gain[...] + merge_bias[...]).astype(bf16)
        grad_rows[rows, :] = norm_backward(cot[rows, :], unit_out, scale_out, merge_gain[...]).astype(bf16)

    send(grad_rows.at[half(0)], grad_rows.at[half(1)], xs.at[0], xr.at[0], pair)

    picker_t = jnp.where(subs == slot_row, 1.0, 0.0).astype(bf16)
    outgoing[...] = jnp.dot(picker_t, merged[...], preferred_element_type=f32).astype(bf16)
    own_slots = pl.ds(pl.multiple_of(d * slot_rows, slot_rows), slot_rows)
    keep = pltpu.make_async_copy(outgoing.at[own_slots], received.at[own_slots], local_sem.at[5])
    keep.start()
    for k in range(1, replicas):
        peer = (d + k) % replicas
        send(
            outgoing.at[pl.ds(pl.multiple_of(peer * slot_rows, slot_rows), slot_rows)],
            received.at[own_slots],
            os_.at[k],
            or_.at[k],
            (s, peer),
        )

    def back(r):
        for b in range(2):
            grad_hidden = jnp.dot(grad_rows[half(r), :], second[b], preferred_element_type=f32)
            grad_pre[b, half(r), :] = (grad_hidden * slope[b, half(r), :]).astype(bf16)

    flip(grad_rows, grad_rows_t, 0)
    back(0)
    arrive(grad_rows.at[half(1)], xr.at[0], xs.at[0])
    flip(grad_rows, grad_rows_t, 1)

    order = list(range(1, chips)) + [0]

    def scatter(w, lhs, rhs):
        def piece(j, b):
            return jnp.dot(lhs[shard_rows(j), :], rhs[b], preferred_element_type=f32)

        for k in order:
            for b in range(2):
                core_out[w, k, b] = piece(chip_at(k) * 2 + mate_core, b).astype(bf16)
            send(core_out.at[w, k], core_in.at[w, k], cs.at[w, k], cr.at[w, k], mate)
        for k in order:
            arrive(core_in.at[w, k], cr.at[w, k], cs.at[w, k])
            for b in range(2):
                value = piece(chip_at(k) * 2 + c, b) + core_in[w, k, b].astype(f32)
                if k:
                    chip_out[w, k, b] = value.astype(bf16)
                else:
                    total[w, b] = value
            if k:
                send(chip_out.at[w, k], chip_in.at[w, k], hs.at[w, k], hr.at[w, k], (s, chip_at(k) * 2 + c))

    def collect(w):
        for k in range(1, chips):
            arrive(chip_in.at[w, k], hr.at[w, k], hs.at[w, k])
        for b in (1, 0):
            value = total[w, b]
            for k in range(1, chips):
                value = value + chip_in[w, k, b].astype(f32)
            if b:
                cross_out[w] = value.astype(bf16)
                send(cross_out.at[w], cross_in.at[w], zs.at[w], zr.at[w], across)
            else:
                total[w, 0] = value

    def finish(w, out):
        arrive(cross_in.at[w], zr.at[w], zs.at[w])
        out[...] = total[w, 0] + cross_in[w].astype(f32)

    scatter(1, grad_rows_t, hidden)
    back(1)
    scatter(0, normed_t, grad_pre)
    collect(1)
    keep.wait()
    for k in range(1, replicas):
        origin = (d + replicas - k) % replicas
        arrive(
            received.at[pl.ds(pl.multiple_of(origin * slot_rows, slot_rows), slot_rows)], or_.at[k], os_.at[k]
        )
    finish(1, grad_out)
    collect(0)
    finish(0, grad_in)
    for copy in sent:
        copy.wait_send()


def in_one_kernel(patches, pre_gain, merge_gain, merge_bias, w_in, w_out, destinations, upstream):
    sections = lax.axis_size("section")
    replicas = lax.axis_size("dp")
    chips = replicas // 2
    share = patches.shape[0] // sections
    features = patches.shape[1]
    merge = upstream.shape[1] // features
    blocks, width = destinations.shape[0], w_in.shape[1]
    shard = w_in.shape[0]
    capacity = upstream.shape[0] // replicas
    f32, bf16 = jnp.float32, jnp.bfloat16
    targets = jnp.repeat(destinations[:, 0], merge).astype(f32)
    block_ids = np.repeat(np.arange(blocks), merge).astype(np.float32)
    member = np.tile(np.arange(merge), blocks).astype(np.float32)
    vmem = pl.BlockSpec(memory_space=pltpu.VMEM)
    hbm = pl.BlockSpec(memory_space=pl.ANY)
    dma = pltpu.SemaphoreType.DMA
    received, grad_in, grad_out_t = pl.pallas_call(
        functools.partial(window_kernel, sections, replicas, merge, capacity),
        out_shape=(
            jax.ShapeDtypeStruct((upstream.shape[0] * merge, features), bf16),
            jax.ShapeDtypeStruct((shard, width), f32),
            jax.ShapeDtypeStruct((shard, width), f32),
        ),
        in_specs=[hbm, vmem, vmem, vmem, hbm, hbm] + [vmem] * 6 + [hbm],
        out_specs=(hbm, vmem, vmem),
        scratch_shapes=[
            pltpu.VMEM((2 * share, features), bf16),
            pltpu.VMEM((2 * share, features), bf16),
            pltpu.VMEM((features, 2 * share), bf16),
            pltpu.VMEM((2, features, width), bf16),
            pltpu.VMEM((2, features, width), bf16),
            pltpu.VMEM((2, 2 * share, width), f32),
            pltpu.VMEM((2, 2 * share, width), bf16),
            pltpu.VMEM((2, share, features // 2), bf16),
            pltpu.VMEM((2, share, features // 2), bf16),
            pltpu.VMEM((share, features), f32),
            pltpu.VMEM((8, 128), f32),
            pltpu.VMEM((share, features), bf16),
            pltpu.VMEM((share, features), bf16),
            pltpu.VMEM((share, features), bf16),
            pltpu.VMEM((share, features), f32),
            pltpu.VMEM((2 * share, features), bf16),
            pltpu.VMEM((features, 2 * share), bf16),
            pltpu.VMEM((2, 2 * share, width), bf16),
            pltpu.VMEM((2, chips, 2, shard, width), bf16),
            pltpu.VMEM((2, chips, 2, shard, width), bf16),
            pltpu.VMEM((2, chips, 2, shard, width), bf16),
            pltpu.VMEM((2, chips, 2, shard, width), bf16),
            pltpu.VMEM((2, 2, shard, width), f32),
            pltpu.VMEM((2, shard, width), bf16),
            pltpu.VMEM((2, shard, width), bf16),
            dma((6,)),
            dma((2, 2, 2 * chips)),
            dma((2, 2, 2 * chips)),
            dma((replicas,)),
            dma((replicas,)),
            dma((replicas,)),
            dma((replicas,)),
            dma((2,)),
            dma((2,)),
            dma((1,)),
            dma((1,)),
            dma((2, chips)),
            dma((2, chips)),
            dma((2, chips)),
            dma((2, chips)),
            dma((2,)),
            dma((2,)),
        ],
        compiler_params=pltpu.CompilerParams(
            collective_id=0, has_side_effects=True, vmem_limit_bytes=60 * 1024 * 1024
        ),
    )(
        patches,
        pre_gain[None, :],
        merge_gain[None, :],
        merge_bias[None, :],
        w_in,
        w_out.T,
        targets[:, None],
        targets[None, :],
        block_ids[:, None],
        block_ids[None, :],
        member[:, None],
        member[None, :],
        upstream.reshape(-1, features),
    )
    return (received.reshape(upstream.shape), grad_in, grad_out_t.T)


def window(*args):
    patches, w_in, upstream = args[0], args[4], args[7]
    sections = lax.axis_size("section")
    replicas = lax.axis_size("dp")
    share = patches.shape[0] // sections
    slots = upstream.shape[0] * upstream.shape[1] // patches.shape[1]
    aligned = w_in.shape[0] % 16 == 0 and w_in.shape[1] % 128 == 0 and patches.shape[1] % 256 == 0
    if aligned and sections == 4 and replicas % 2 == 0 and slots == share:
        return in_one_kernel(*args)
    return on_device(*args)


def solution(mesh):
    return jax.shard_map(
        window,
        mesh=mesh,
        in_specs=(
            P("dp", None),
            P(),
            P(),
            P(),
            P("dp", "section"),
            P("section", "dp"),
            P(("section", "dp"), None),
            P(("section", "dp"), None),
        ),
        out_specs=(P(("section", "dp"), None), P("dp", "section"), P("section", "dp")),
        check_vma=False,
    )
```

```python
import functools

import jax
import jax.numpy as jnp
import numpy as np
from jax import lax
from jax.experimental import pallas as pl
from jax.experimental.pallas import tpu as pltpu
from jax.sharding import PartitionSpec as P

BLK = 1


epsilon = 1e-06
gelu_scale = 0.7978845608028654
gelu_cubic = 0.044715


def gelu_slope(values):
    tangent = jnp.tanh(gelu_scale * (values + gelu_cubic * values * values * values))
    return 0.5 * (1.0 + tangent) + 0.5 * values * (1.0 - tangent * tangent) * gelu_scale * (
        1.0 + 3.0 * gelu_cubic * values * values
    )


def normalize(values):
    average = jnp.mean(values, axis=-1, keepdims=True)
    centred = values - average
    inv_scale = lax.rsqrt(jnp.mean(centred * centred, axis=-1, keepdims=True) + epsilon)
    return (centred * inv_scale, inv_scale)


def norm_backward(cotangent, unit_rows, inv_scale, gain):
    scaled = cotangent * gain
    return inv_scale * (
        scaled
        - jnp.mean(scaled, axis=-1, keepdims=True)
        - unit_rows * jnp.mean(scaled * unit_rows, axis=-1, keepdims=True)
    )


def block_ranks(targets):
    block_count = targets.shape[-1]
    matches = targets[:, None] == targets[None, :]
    earlier = lax.broadcasted_iota(jnp.int32, (block_count, block_count), 1) < lax.broadcasted_iota(
        jnp.int32, (block_count, block_count), 0
    )
    return jnp.sum((matches & earlier).astype(jnp.int32), axis=-1)


def on_device(patches, pre_gain, merge_gain, merge_bias, w_in, w_out, destinations, upstream):
    sections = lax.axis_size("section")
    replicas = lax.axis_size("dp")
    group_rows = patches.shape[0]
    share_rows = group_rows // sections
    feature_count = patches.shape[1]
    merged_width = upstream.shape[1]
    block_width = BLK * merged_width
    block_count = destinations.shape[0]
    capacity = upstream.shape[0] // (replicas * BLK)
    inputs = patches.astype(jnp.float32)
    unit_rows, _ = normalize(inputs)
    normed = (unit_rows * pre_gain).astype(jnp.bfloat16)
    preact = jnp.dot(
        normed, lax.all_gather(w_in, "dp", axis=0, tiled=True), preferred_element_type=jnp.float32
    )
    hidden = jax.nn.gelu(preact, approximate=True).astype(jnp.bfloat16)
    out_full = lax.all_gather(w_out, "dp", axis=1, tiled=True)
    partial_value = jnp.dot(hidden, out_full, preferred_element_type=jnp.float32).astype(jnp.bfloat16)
    row_start = lax.axis_index("section") * share_rows
    own_inputs = lax.dynamic_slice_in_dim(inputs, row_start, share_rows, 0)
    residual = own_inputs + lax.psum_scatter(
        partial_value, "section", scatter_dimension=0, tiled=True
    ).astype(jnp.float32)
    unit_out, scale_out = normalize(residual)
    merged = (unit_out * merge_gain + merge_bias).astype(jnp.bfloat16)
    blocks = merged.reshape(block_count, block_width)
    targets = destinations[:, 0]
    block_rank = block_ranks(targets)
    column_ids = lax.broadcasted_iota(jnp.int32, (block_count, replicas * capacity), 1)
    picker = ((targets * capacity + block_rank)[:, None] == column_ids).astype(jnp.bfloat16)
    outgoing = lax.dot_general(
        picker, blocks, (((0,), (0,)), ((), ())), preferred_element_type=jnp.float32
    ).astype(jnp.bfloat16)
    arrived = lax.all_to_all(
        outgoing.reshape(replicas, capacity * block_width),
        "dp",
        split_axis=0,
        concat_axis=0,
        tiled=True,
    )
    received = arrived.reshape(replicas * capacity * BLK, merged_width)
    coming = lax.all_to_all(
        upstream.reshape(replicas, capacity * block_width),
        "dp",
        split_axis=0,
        concat_axis=0,
        tiled=True,
    )
    cotangent = jnp.dot(
        picker, coming.reshape(replicas * capacity, block_width), preferred_element_type=jnp.float32
    )
    cotangent = cotangent.astype(jnp.bfloat16).reshape(share_rows, feature_count)
    grad_own = norm_backward(cotangent.astype(jnp.float32), unit_out, scale_out, merge_gain).astype(
        jnp.bfloat16
    )
    grad_residual = lax.all_gather(grad_own, "section", axis=0, tiled=True)
    grad_second = lax.dot_general(
        hidden, grad_residual, (((0,), (0,)), ((), ())), preferred_element_type=jnp.float32
    )
    grad_hidden = lax.dot_general(
        grad_residual, out_full, (((1,), (1,)), ((), ())), preferred_element_type=jnp.float32
    )
    grad_preact = (grad_hidden * gelu_slope(preact)).astype(jnp.bfloat16)
    grad_first = lax.dot_general(
        normed, grad_preact, (((0,), (0,)), ((), ())), preferred_element_type=jnp.float32
    )
    grad_w_in, grad_w_out = (
        lax.psum_scatter(grad_first.astype(jnp.bfloat16), "dp", scatter_dimension=0, tiled=True).astype(jnp.float32),
        lax.psum_scatter(grad_second.astype(jnp.bfloat16), "dp", scatter_dimension=1, tiled=True).astype(jnp.float32),
    )
    return (received, grad_w_in, grad_w_out)


TILE = 32


def remote(src, dst, send_sem, recv_sem, device):
    return pltpu.make_async_remote_copy(
        src_ref=src,
        dst_ref=dst,
        send_sem=send_sem,
        recv_sem=recv_sem,
        device_id=device,
        device_id_type=pl.DeviceIdType.MESH,
    )


def window_kernel(
    sections, replicas, merge, capacity,
    patches, pre_gain, merge_gain, merge_bias, w_in, w_out_t, tcol, trow, bcol, brow, mcol, mrow, upstream,
    received, grad_in, grad_out,
    rows_in, normed, normed_t, first, second, slope, hidden, part_out, part_in, unit, inv, merged, outgoing,
    coming, cot, grad_rows, grad_rows_t, grad_pre, core_out, core_in, chip_out, chip_in, total, cross_out,
    cross_in, local_sem, gs, gr, us, ur, os_, or_, ps, pr, xs, xr, cs, cr, hs, hr, zs, zr,
):
    share = rows_in.shape[0] // 2
    features = rows_in.shape[1]
    width = w_in.shape[1]
    shard = w_in.shape[0]
    chips = replicas // 2
    f32, bf16 = jnp.float32, jnp.bfloat16
    s, d = lax.axis_index("section"), lax.axis_index("dp")
    q, c = d // 2, d % 2
    pair = (s + 1 - 2 * (s % 2), d)
    across = ((s + sections // 2) % sections, d)
    mate_core = 1 - c
    mate = (s, q * 2 + mate_core)

    beside, below = q + 1 - 2 * (q % 2), (q + 2) % chips
    corner = (beside + 2) % chips

    def side(b):
        return (below, beside) if b == 0 else (beside, below)

    def shard_rows(j):
        return pl.ds(pl.multiple_of(j * shard, 16), shard)

    sent = []

    def send(*args):
        copy = remote(*args)
        copy.start()
        sent.append(copy)

    def arrive(dst, recv_sem, send_sem):
        remote(dst, dst, send_sem, recv_sem, mate).wait_recv()

    shards, fulls = (w_in, w_out_t), (first, second)
    loads = [
        pltpu.make_async_copy(
            patches.at[pl.ds(pl.multiple_of(s * share, share), share)], rows_in.at[pl.ds(0, share)], local_sem.at[0]
        ),
        pltpu.make_async_copy(
            patches.at[pl.ds(pl.multiple_of(pair[0] * share, share), share)],
            rows_in.at[pl.ds(share, share)],
            local_sem.at[1],
        ),
        pltpu.make_async_copy(w_in, first.at[0, shard_rows(d)], local_sem.at[2]),
        pltpu.make_async_copy(w_out_t, second.at[0, shard_rows(d)], local_sem.at[3]),
    ]
    slot_rows = capacity * merge
    loads.append(
        pltpu.make_async_copy(
            upstream.at[pl.ds(pl.multiple_of(d * slot_rows, slot_rows), slot_rows)],
            coming.at[pl.ds(pl.multiple_of(d * slot_rows, slot_rows), slot_rows)],
            local_sem.at[4],
        )
    )
    for copy in loads:
        copy.start()

    barrier = pltpu.get_barrier_semaphore()
    for k in range(1, replicas):
        pl.semaphore_signal(
            barrier, inc=1, device_id=(s, (d + k) % replicas), device_id_type=pl.DeviceIdType.MESH
        )
    for peer in (pair, across):
        pl.semaphore_signal(barrier, inc=1, device_id=peer, device_id_type=pl.DeviceIdType.MESH)
    pl.semaphore_wait(barrier, replicas + 1)

    for w in range(2):
        send(shards[w], fulls[w].at[1, shard_rows(d)], gs.at[w, 1, 0], gr.at[w, 1, 0], across)

    def spread(w, b):
        src = shards[w] if b == 0 else fulls[w].at[1, shard_rows(d)]
        place = fulls[w].at[b, shard_rows(d)]
        peers = [(s, chip * 2 + c) for chip in side(b)] + [mate]
        for slot, peer in enumerate(peers, 1):
            send(src, place, gs.at[w, b, slot], gr.at[w, b, slot], peer)

    def origin_of(b, slot):
        return {1: side(b)[0], 2: side(b)[1], 4: corner}[slot]

    def got(w, b, slot):
        place = fulls[w].at[b, shard_rows(origin_of(b, slot) * 2 + c)]
        arrive(place, gr.at[w, b, slot], gs.at[w, b, slot])
        if slot == 1:
            send(place, place, gs.at[w, b, 4], gr.at[w, b, 4], (s, side(b)[1] * 2 + c))
        to_mate = {1: 5, 2: 6, 4: 7}[slot]
        send(place, place, gs.at[w, b, to_mate], gr.at[w, b, to_mate], mate)

    def from_mate(w, b, slot):
        chip = q if slot == 3 else origin_of(b, {5: 1, 6: 2, 7: 4}[slot])
        arrive(fulls[w].at[b, shard_rows(chip * 2 + mate_core)], gr.at[w, b, slot], gs.at[w, b, slot])

    spread(0, 0)
    arrive(first.at[1, shard_rows(d)], gr.at[0, 1, 0], gs.at[0, 1, 0])
    spread(0, 1)
    got(0, 0, 1)
    spread(1, 0)
    got(0, 1, 1)
    arrive(second.at[1, shard_rows(d)], gr.at[1, 1, 0], gs.at[1, 1, 0])
    spread(1, 1)

    for copy in loads:
        copy.wait()

    def tile_rows(i):
        return pl.ds(pl.multiple_of(i * TILE, TILE), TILE)

    @pl.loop(0, 2 * share // TILE)
    def _(i):
        unit_rows, _ = normalize(rows_in[tile_rows(i), :].astype(f32))
        normed[tile_rows(i), :] = (unit_rows * pre_gain[...][None, :]).astype(bf16)

    def flip(src, dst, r):
        @pl.loop(0, features // 128)
        def _(i):
            cols = pl.ds(pl.multiple_of(i * 128, 128), 128)
            dst[cols, pl.ds(r * share, share)] = src[pl.ds(r * share, share), cols].T

    got(0, 0, 2)
    got(0, 1, 2)
    got(1, 0, 1)
    flip(normed, normed_t, 0)
    got(0, 0, 4)
    got(0, 1, 4)
    flip(normed, normed_t, 1)
    got(1, 1, 1)
    for k in range(1, replicas):
        peer = (d + k) % replicas
        send(
            upstream.at[pl.ds(pl.multiple_of(peer * slot_rows, slot_rows), slot_rows)],
            coming.at[pl.ds(pl.multiple_of(d * slot_rows, slot_rows), slot_rows)],
            us.at[k],
            ur.at[k],
            (s, peer),
        )

    matches = tcol[...] == trow[...]
    above = jnp.where(matches & (brow[...] < bcol[...]) & (mrow[...] == 0.0), 1.0, 0.0)
    left = jnp.where(matches & (bcol[...] < brow[...]) & (mcol[...] == 0.0), 1.0, 0.0)
    slot_col = (tcol[...] * capacity + jnp.sum(above, axis=1, keepdims=True)) * merge + mcol[...]
    slot_row = (trow[...] * capacity + jnp.sum(left, axis=0, keepdims=True)) * merge + mrow[...]
    lanes = lax.broadcasted_iota(jnp.int32, (share, share), 1).astype(f32)
    subs = lax.broadcasted_iota(jnp.int32, (share, share), 0).astype(f32)

    def half(r):
        return pl.ds(r * share, share)

    for b in range(2):
        for slot in (3, 5, 6, 7):
            from_mate(0, b, slot)
        for r in range(2):
            slope[b, half(r), :] = jnp.dot(normed[half(r), :], first[b], preferred_element_type=f32)
        if b == 0:
            got(1, 0, 2)
            got(1, 1, 2)

        @pl.loop(0, 2 * share // TILE)
        def _(i):
            u = slope[b, tile_rows(i), :]
            tangent = jnp.tanh(gelu_scale * (u + gelu_cubic * u * u * u))
            hidden[b, tile_rows(i), :] = (0.5 * u * (1.0 + tangent)).astype(bf16)
            slope[b, tile_rows(i), :] = 0.5 * (1.0 + tangent) + 0.5 * u * (1.0 - tangent * tangent) * gelu_scale * (
                1.0 + 3.0 * gelu_cubic * u * u
            )

    nt = (((1,), (1,)), ((), ()))
    split = features // 2

    def project(r, h):
        value = 0.0
        for b in range(2):
            value = value + lax.dot_general(
                hidden[b, half(r), :],
                second[b, pl.ds(pl.multiple_of(h * split, 128), split), :],
                nt,
                preferred_element_type=f32,
            )
        return value

    near = q // 2
    for step, h in enumerate((near, 1 - near)):
        if step == 0:
            for b, slot in ((0, 3), (1, 3), (0, 6), (1, 5)):
                from_mate(1, b, slot)
        else:
            got(1, 0, 4)
            got(1, 1, 4)
            for b, slot in ((0, 5), (1, 6), (0, 7), (1, 7)):
                from_mate(1, b, slot)
        part_out[h] = project(1, h).astype(bf16)
        send(part_out.at[h], part_in.at[h], ps.at[step], pr.at[step], pair)
    for h in range(2):
        unit[:, pl.ds(h * split, split)] = project(0, h)

    for k in range(1, replicas):
        origin = (d + replicas - k) % replicas
        arrive(
            coming.at[pl.ds(pl.multiple_of(origin * slot_rows, slot_rows), slot_rows)], ur.at[k], us.at[k]
        )
    picker = jnp.where(slot_col == lanes, 1.0, 0.0).astype(bf16)
    cot[...] = jnp.dot(picker, coming[...], preferred_element_type=f32)
    for step, h in enumerate((near, 1 - near)):
        arrive(part_in.at[h], pr.at[step], ps.at[step])

    @pl.loop(0, share // TILE)
    def _(i):
        rows = tile_rows(i)
        partner = jnp.concatenate([part_in[h, rows, :].astype(f32) for h in range(2)], axis=1)
        residual = rows_in[rows, :].astype(f32) + (unit[rows, :] + partner)
        unit_out, scale_out = normalize(residual)
        merged[rows, :] = (unit_out * merge_gain[...][None, :] + merge_bias[...][None, :]).astype(bf16)
        grad_rows[rows, :] = norm_backward(cot[rows, :], unit_out, scale_out, merge_gain[...][None, :]).astype(bf16)

    send(grad_rows.at[half(0)], grad_rows.at[half(1)], xs.at[0], xr.at[0], pair)

    picker_t = jnp.where(subs == slot_row, 1.0, 0.0).astype(bf16)
    outgoing[...] = jnp.dot(picker_t, merged[...], preferred_element_type=f32).astype(bf16)
    own_slots = pl.ds(pl.multiple_of(d * slot_rows, slot_rows), slot_rows)
    keep = pltpu.make_async_copy(outgoing.at[own_slots], received.at[own_slots], local_sem.at[5])
    keep.start()
    for k in range(1, replicas):
        peer = (d + k) % replicas
        send(
            outgoing.at[pl.ds(pl.multiple_of(peer * slot_rows, slot_rows), slot_rows)],
            received.at[own_slots],
            os_.at[k],
            or_.at[k],
            (s, peer),
        )

    def back(r):
        for b in range(2):
            grad_hidden = jnp.dot(grad_rows[half(r), :], second[b], preferred_element_type=f32)
            grad_pre[b, half(r), :] = (grad_hidden * slope[b, half(r), :]).astype(bf16)

    flip(grad_rows, grad_rows_t, 0)
    back(0)
    arrive(grad_rows.at[half(1)], xr.at[0], xs.at[0])
    flip(grad_rows, grad_rows_t, 1)

    def piece(w, j, b):
        lhs, rhs = ((normed_t, grad_pre), (grad_rows_t, hidden))[w]
        return jnp.dot(lhs[shard_rows(j), :], rhs[b], preferred_element_type=f32)

    def both_cores(w, b, k, chip):
        value = piece(w, chip * 2 + c, b)
        arrive(core_in.at[w, b, k], cr.at[w, b, k], cs.at[w, b, k])
        return value + core_in[w, b, k].astype(f32)

    def pass_on(w, b, k, value, chip):
        chip_out[w, b, k] = value.astype(bf16)
        send(chip_out.at[w, b, k], chip_in.at[w, b, k], hs.at[w, b, k], hr.at[w, b, k], (s, chip * 2 + c))

    def taken(w, b, k):
        arrive(chip_in.at[w, b, k], hr.at[w, b, k], hs.at[w, b, k])
        return chip_in[w, b, k].astype(f32)

    def begin(w, b):
        lead, follow = side(b)
        for k, chip in enumerate((corner, lead, follow, q)):
            core_out[w, b, k] = piece(w, chip * 2 + mate_core, b).astype(bf16)
            send(core_out.at[w, b, k], core_in.at[w, b, k], cs.at[w, b, k], cr.at[w, b, k], mate)
        pass_on(w, b, 0, both_cores(w, b, 0, corner), lead)
        pass_on(w, b, 1, both_cores(w, b, 1, lead), lead)

    def middle(w, b):
        follow = side(b)[1]
        value = both_cores(w, b, 2, follow)
        pass_on(w, b, 2, value + taken(w, b, 0), follow)
        total[w, b] = both_cores(w, b, 3, q)

    def close(w, b):
        value = total[w, b] + taken(w, b, 1)
        value = value + taken(w, b, 2)
        if b:
            cross_out[w] = value.astype(bf16)
            send(cross_out.at[w], cross_in.at[w], zs.at[w], zr.at[w], across)
        else:
            total[w, 0] = value

    def finish(w, out):
        arrive(cross_in.at[w], zr.at[w], zs.at[w])
        out[...] = total[w, 0] + cross_in[w].astype(f32)

    begin(1, 1)
    begin(1, 0)
    back(1)
    middle(1, 1)
    begin(0, 1)
    middle(1, 0)
    begin(0, 0)
    close(1, 1)
    middle(0, 1)
    close(1, 0)
    middle(0, 0)
    close(0, 1)
    keep.wait()
    for k in range(1, replicas):
        origin = (d + replicas - k) % replicas
        arrive(
            received.at[pl.ds(pl.multiple_of(origin * slot_rows, slot_rows), slot_rows)], or_.at[k], os_.at[k]
        )
    finish(1, grad_out)
    close(0, 0)
    finish(0, grad_in)
    for copy in sent:
        copy.wait_send()


def in_one_kernel(patches, pre_gain, merge_gain, merge_bias, w_in, w_out, destinations, upstream):
    sections = lax.axis_size("section")
    replicas = lax.axis_size("dp")
    chips = replicas // 2
    share = patches.shape[0] // sections
    features = patches.shape[1]
    merge = upstream.shape[1] // features
    blocks, width = destinations.shape[0], w_in.shape[1]
    shard = w_in.shape[0]
    capacity = upstream.shape[0] // replicas
    f32, bf16 = jnp.float32, jnp.bfloat16
    targets = jnp.repeat(destinations[:, 0], merge).astype(f32)
    block_ids = np.repeat(np.arange(blocks), merge).astype(np.float32)
    member = np.tile(np.arange(merge), blocks).astype(np.float32)
    vmem = pl.BlockSpec(memory_space=pltpu.VMEM)
    hbm = pl.BlockSpec(memory_space=pl.ANY)
    dma = pltpu.SemaphoreType.DMA
    received, grad_in, grad_out_t = pl.pallas_call(
        functools.partial(window_kernel, sections, replicas, merge, capacity),
        out_shape=(
            jax.ShapeDtypeStruct((upstream.shape[0] * merge, features), bf16),
            jax.ShapeDtypeStruct((shard, width), f32),
            jax.ShapeDtypeStruct((shard, width), f32),
        ),
        in_specs=[hbm, vmem, vmem, vmem, hbm, hbm] + [vmem] * 6 + [hbm],
        out_specs=(hbm, vmem, vmem),
        scratch_shapes=[
            pltpu.VMEM((2 * share, features), bf16),
            pltpu.VMEM((2 * share, features), bf16),
            pltpu.VMEM((features, 2 * share), bf16),
            pltpu.VMEM((2, features, width), bf16),
            pltpu.VMEM((2, features, width), bf16),
            pltpu.VMEM((2, 2 * share, width), f32),
            pltpu.VMEM((2, 2 * share, width), bf16),
            pltpu.VMEM((2, share, features // 2), bf16),
            pltpu.VMEM((2, share, features // 2), bf16),
            pltpu.VMEM((share, features), f32),
            pltpu.VMEM((8, 128), f32),
            pltpu.VMEM((share, features), bf16),
            pltpu.VMEM((share, features), bf16),
            pltpu.VMEM((share, features), bf16),
            pltpu.VMEM((share, features), f32),
            pltpu.VMEM((2 * share, features), bf16),
            pltpu.VMEM((features, 2 * share), bf16),
            pltpu.VMEM((2, 2 * share, width), bf16),
            pltpu.VMEM((2, 2, chips, shard, width), bf16),
            pltpu.VMEM((2, 2, chips, shard, width), bf16),
            pltpu.VMEM((2, 2, chips - 1, shard, width), bf16),
            pltpu.VMEM((2, 2, chips - 1, shard, width), bf16),
            pltpu.VMEM((2, 2, shard, width), f32),
            pltpu.VMEM((2, shard, width), bf16),
            pltpu.VMEM((2, shard, width), bf16),
            dma((6,)),
            dma((2, 2, 2 * chips)),
            dma((2, 2, 2 * chips)),
            dma((replicas,)),
            dma((replicas,)),
            dma((replicas,)),
            dma((replicas,)),
            dma((2,)),
            dma((2,)),
            dma((1,)),
            dma((1,)),
            dma((2, 2, chips)),
            dma((2, 2, chips)),
            dma((2, 2, chips - 1)),
            dma((2, 2, chips - 1)),
            dma((2,)),
            dma((2,)),
        ],
        compiler_params=pltpu.CompilerParams(
            collective_id=0, has_side_effects=True, vmem_limit_bytes=60 * 1024 * 1024
        ),
    )(
        patches,
        pre_gain,
        merge_gain,
        merge_bias,
        w_in,
        w_out.T,
        targets[:, None],
        targets[None, :],
        block_ids[:, None],
        block_ids[None, :],
        member[:, None],
        member[None, :],
        upstream.reshape(-1, features),
    )
    return (received.reshape(upstream.shape), grad_in, grad_out_t.T)


def window(*args):
    patches, w_in, upstream = args[0], args[4], args[7]
    sections = lax.axis_size("section")
    replicas = lax.axis_size("dp")
    share = patches.shape[0] // sections
    slots = upstream.shape[0] * upstream.shape[1] // patches.shape[1]
    aligned = w_in.shape[0] % 16 == 0 and w_in.shape[1] % 128 == 0 and patches.shape[1] % 256 == 0
    if aligned and sections == 4 and replicas == 8 and slots == share:
        return in_one_kernel(*args)
    return on_device(*args)


def solution(mesh):
    return jax.shard_map(
        window,
        mesh=mesh,
        in_specs=(
            P("dp", None),
            P(),
            P(),
            P(),
            P("dp", "section"),
            P("section", "dp"),
            P(("section", "dp"), None),
            P(("section", "dp"), None),
        ),
        out_specs=(P(("section", "dp"), None), P("dp", "section"), P("section", "dp")),
        check_vma=False,
    )
```

```python
import functools

import jax
import jax.numpy as jnp
import numpy as np
from jax import lax
from jax.experimental import pallas as pl
from jax.experimental.pallas import tpu as pltpu
from jax.sharding import PartitionSpec as P

BLK = 1


epsilon = 1e-06
gelu_scale = 0.7978845608028654
gelu_cubic = 0.044715


def gelu_slope(values):
    tangent = jnp.tanh(gelu_scale * (values + gelu_cubic * values * values * values))
    return 0.5 * (1.0 + tangent) + 0.5 * values * (1.0 - tangent * tangent) * gelu_scale * (
        1.0 + 3.0 * gelu_cubic * values * values
    )


def normalize(values):
    average = jnp.mean(values, axis=-1, keepdims=True)
    centred = values - average
    inv_scale = lax.rsqrt(jnp.mean(centred * centred, axis=-1, keepdims=True) + epsilon)
    return (centred * inv_scale, inv_scale)


def norm_backward(cotangent, unit_rows, inv_scale, gain):
    scaled = cotangent * gain
    return inv_scale * (
        scaled
        - jnp.mean(scaled, axis=-1, keepdims=True)
        - unit_rows * jnp.mean(scaled * unit_rows, axis=-1, keepdims=True)
    )


def block_ranks(targets):
    block_count = targets.shape[-1]
    matches = targets[:, None] == targets[None, :]
    earlier = lax.broadcasted_iota(jnp.int32, (block_count, block_count), 1) < lax.broadcasted_iota(
        jnp.int32, (block_count, block_count), 0
    )
    return jnp.sum((matches & earlier).astype(jnp.int32), axis=-1)


def on_device(patches, pre_gain, merge_gain, merge_bias, w_in, w_out, destinations, upstream):
    sections = lax.axis_size("section")
    replicas = lax.axis_size("dp")
    group_rows = patches.shape[0]
    share_rows = group_rows // sections
    feature_count = patches.shape[1]
    merged_width = upstream.shape[1]
    block_width = BLK * merged_width
    block_count = destinations.shape[0]
    capacity = upstream.shape[0] // (replicas * BLK)
    inputs = patches.astype(jnp.float32)
    unit_rows, _ = normalize(inputs)
    normed = (unit_rows * pre_gain).astype(jnp.bfloat16)
    preact = jnp.dot(
        normed, lax.all_gather(w_in, "dp", axis=0, tiled=True), preferred_element_type=jnp.float32
    )
    hidden = jax.nn.gelu(preact, approximate=True).astype(jnp.bfloat16)
    out_full = lax.all_gather(w_out, "dp", axis=1, tiled=True)
    partial_value = jnp.dot(hidden, out_full, preferred_element_type=jnp.float32).astype(jnp.bfloat16)
    row_start = lax.axis_index("section") * share_rows
    own_inputs = lax.dynamic_slice_in_dim(inputs, row_start, share_rows, 0)
    residual = own_inputs + lax.psum_scatter(
        partial_value, "section", scatter_dimension=0, tiled=True
    ).astype(jnp.float32)
    unit_out, scale_out = normalize(residual)
    merged = (unit_out * merge_gain + merge_bias).astype(jnp.bfloat16)
    blocks = merged.reshape(block_count, block_width)
    targets = destinations[:, 0]
    block_rank = block_ranks(targets)
    column_ids = lax.broadcasted_iota(jnp.int32, (block_count, replicas * capacity), 1)
    picker = ((targets * capacity + block_rank)[:, None] == column_ids).astype(jnp.bfloat16)
    outgoing = lax.dot_general(
        picker, blocks, (((0,), (0,)), ((), ())), preferred_element_type=jnp.float32
    ).astype(jnp.bfloat16)
    arrived = lax.all_to_all(
        outgoing.reshape(replicas, capacity * block_width),
        "dp",
        split_axis=0,
        concat_axis=0,
        tiled=True,
    )
    received = arrived.reshape(replicas * capacity * BLK, merged_width)
    coming = lax.all_to_all(
        upstream.reshape(replicas, capacity * block_width),
        "dp",
        split_axis=0,
        concat_axis=0,
        tiled=True,
    )
    cotangent = jnp.dot(
        picker, coming.reshape(replicas * capacity, block_width), preferred_element_type=jnp.float32
    )
    cotangent = cotangent.astype(jnp.bfloat16).reshape(share_rows, feature_count)
    grad_own = norm_backward(cotangent.astype(jnp.float32), unit_out, scale_out, merge_gain).astype(
        jnp.bfloat16
    )
    grad_residual = lax.all_gather(grad_own, "section", axis=0, tiled=True)
    grad_second = lax.dot_general(
        hidden, grad_residual, (((0,), (0,)), ((), ())), preferred_element_type=jnp.float32
    )
    grad_hidden = lax.dot_general(
        grad_residual, out_full, (((1,), (1,)), ((), ())), preferred_element_type=jnp.float32
    )
    grad_preact = (grad_hidden * gelu_slope(preact)).astype(jnp.bfloat16)
    grad_first = lax.dot_general(
        normed, grad_preact, (((0,), (0,)), ((), ())), preferred_element_type=jnp.float32
    )
    grad_w_in, grad_w_out = (
        lax.psum_scatter(grad_first.astype(jnp.bfloat16), "dp", scatter_dimension=0, tiled=True).astype(jnp.float32),
        lax.psum_scatter(grad_second.astype(jnp.bfloat16), "dp", scatter_dimension=1, tiled=True).astype(jnp.float32),
    )
    return (received, grad_w_in, grad_w_out)


TILE = 32


def remote(src, dst, send_sem, recv_sem, device):
    return pltpu.make_async_remote_copy(
        src_ref=src,
        dst_ref=dst,
        send_sem=send_sem,
        recv_sem=recv_sem,
        device_id=device,
        device_id_type=pl.DeviceIdType.MESH,
    )


def window_kernel(
    sections, replicas, merge, capacity,
    patches, pre_gain, merge_gain, merge_bias, w_in, w_out_t, tcol, trow, bcol, brow, mcol, mrow, upstream,
    received, grad_in, grad_out,
    rows_in, normed, normed_t, first, second, slope, hidden, part_out, part_in, unit, inv, merged, outgoing,
    coming, cot, grad_rows, grad_rows_t, grad_pre, core_out, core_in, chip_out, chip_in, total, cross_out,
    cross_in, local_sem, gs, gr, us, ur, os_, or_, ps, pr, xs, xr, cs, cr, hs, hr, zs, zr,
):
    share = rows_in.shape[0] // 2
    features = rows_in.shape[1]
    width = w_in.shape[1]
    shard = w_in.shape[0]
    chips = replicas // 2
    f32, bf16 = jnp.float32, jnp.bfloat16
    s, d = lax.axis_index("section"), lax.axis_index("dp")
    q, c = d // 2, d % 2
    pair = (s + 1 - 2 * (s % 2), d)
    across = ((s + sections // 2) % sections, d)
    mate_core = 1 - c
    mate = (s, q * 2 + mate_core)

    beside, below = q + 1 - 2 * (q % 2), (q + 2) % chips
    corner = (beside + 2) % chips

    def side(w, b):
        return (below, beside) if w == b else (beside, below)

    def shard_rows(j):
        return pl.ds(pl.multiple_of(j * shard, 16), shard)

    sent = []

    def send(*args):
        copy = remote(*args)
        copy.start()
        sent.append(copy)

    def arrive(dst, recv_sem, send_sem):
        remote(dst, dst, send_sem, recv_sem, mate).wait_recv()

    shards, fulls = (w_in, w_out_t), (first, second)
    loads = [
        pltpu.make_async_copy(
            patches.at[pl.ds(pl.multiple_of(s * share, share), share)], rows_in.at[pl.ds(0, share)], local_sem.at[0]
        ),
        pltpu.make_async_copy(
            patches.at[pl.ds(pl.multiple_of(pair[0] * share, share), share)],
            rows_in.at[pl.ds(share, share)],
            local_sem.at[1],
        ),
        pltpu.make_async_copy(w_in, first.at[0, shard_rows(d)], local_sem.at[2]),
        pltpu.make_async_copy(w_out_t, second.at[0, shard_rows(d)], local_sem.at[3]),
    ]
    slot_rows = capacity * merge
    loads.append(
        pltpu.make_async_copy(
            upstream.at[pl.ds(pl.multiple_of(d * slot_rows, slot_rows), slot_rows)],
            coming.at[pl.ds(pl.multiple_of(d * slot_rows, slot_rows), slot_rows)],
            local_sem.at[4],
        )
    )
    for copy in loads:
        copy.start()

    barrier = pltpu.get_barrier_semaphore()
    for k in range(1, replicas):
        pl.semaphore_signal(
            barrier, inc=1, device_id=(s, (d + k) % replicas), device_id_type=pl.DeviceIdType.MESH
        )
    for peer in (pair, across):
        pl.semaphore_signal(barrier, inc=1, device_id=peer, device_id_type=pl.DeviceIdType.MESH)
    pl.semaphore_wait(barrier, replicas + 1)

    for w in range(2):
        send(shards[w], fulls[w].at[1, shard_rows(d)], gs.at[w, 1, 0], gr.at[w, 1, 0], across)

    def spread(w, b):
        src = shards[w] if b == 0 else fulls[w].at[1, shard_rows(d)]
        place = fulls[w].at[b, shard_rows(d)]
        peers = [(s, chip * 2 + c) for chip in side(w, b)] + [mate]
        for slot, peer in enumerate(peers, 1):
            send(src, place, gs.at[w, b, slot], gr.at[w, b, slot], peer)

    def origin_of(w, b, slot):
        return {1: side(w, b)[0], 2: side(w, b)[1], 4: corner}[slot]

    def got(w, b, slot):
        place = fulls[w].at[b, shard_rows(origin_of(w, b, slot) * 2 + c)]
        arrive(place, gr.at[w, b, slot], gs.at[w, b, slot])
        if slot == 1:
            send(place, place, gs.at[w, b, 4], gr.at[w, b, 4], (s, side(w, b)[1] * 2 + c))
        to_mate = {1: 5, 2: 6, 4: 7}[slot]
        send(place, place, gs.at[w, b, to_mate], gr.at[w, b, to_mate], mate)

    def from_mate(w, b, slot):
        chip = q if slot == 3 else origin_of(w, b, {5: 1, 6: 2, 7: 4}[slot])
        arrive(fulls[w].at[b, shard_rows(chip * 2 + mate_core)], gr.at[w, b, slot], gs.at[w, b, slot])

    spread(0, 0)
    spread(1, 0)
    got(0, 0, 1)
    got(1, 0, 1)
    arrive(first.at[1, shard_rows(d)], gr.at[0, 1, 0], gs.at[0, 1, 0])
    spread(0, 1)
    arrive(second.at[1, shard_rows(d)], gr.at[1, 1, 0], gs.at[1, 1, 0])
    spread(1, 1)

    for copy in loads:
        copy.wait()

    def tile_rows(i):
        return pl.ds(pl.multiple_of(i * TILE, TILE), TILE)

    @pl.loop(0, 2 * share // TILE)
    def _(i):
        unit_rows, _ = normalize(rows_in[tile_rows(i), :].astype(f32))
        normed[tile_rows(i), :] = (unit_rows * pre_gain[...][None, :]).astype(bf16)

    def flip(src, dst, r):
        @pl.loop(0, features // 128)
        def _(i):
            cols = pl.ds(pl.multiple_of(i * 128, 128), 128)
            dst[cols, pl.ds(r * share, share)] = src[pl.ds(r * share, share), cols].T

    got(0, 0, 2)
    got(0, 0, 4)
    got(0, 1, 1)
    got(1, 1, 1)
    flip(normed, normed_t, 0)
    flip(normed, normed_t, 1)
    for k in range(1, replicas):
        peer = (d + k) % replicas
        send(
            upstream.at[pl.ds(pl.multiple_of(peer * slot_rows, slot_rows), slot_rows)],
            coming.at[pl.ds(pl.multiple_of(d * slot_rows, slot_rows), slot_rows)],
            us.at[k],
            ur.at[k],
            (s, peer),
        )

    matches = tcol[...] == trow[...]
    above = jnp.where(matches & (brow[...] < bcol[...]) & (mrow[...] == 0.0), 1.0, 0.0)
    left = jnp.where(matches & (bcol[...] < brow[...]) & (mcol[...] == 0.0), 1.0, 0.0)
    slot_col = (tcol[...] * capacity + jnp.sum(above, axis=1, keepdims=True)) * merge + mcol[...]
    slot_row = (trow[...] * capacity + jnp.sum(left, axis=0, keepdims=True)) * merge + mrow[...]
    lanes = lax.broadcasted_iota(jnp.int32, (share, share), 1).astype(f32)
    subs = lax.broadcasted_iota(jnp.int32, (share, share), 0).astype(f32)

    def half(r):
        return pl.ds(r * share, share)

    for b in range(2):
        if b == 1:
            got(0, 1, 2)
            got(0, 1, 4)
        for slot in (3, 5, 6, 7):
            from_mate(0, b, slot)
        for r in range(2):
            slope[b, half(r), :] = jnp.dot(normed[half(r), :], first[b], preferred_element_type=f32)
        if b == 0:
            got(1, 0, 2)
            got(1, 1, 2)

        @pl.loop(0, 2 * share // TILE)
        def _(i):
            u = slope[b, tile_rows(i), :]
            tangent = jnp.tanh(gelu_scale * (u + gelu_cubic * u * u * u))
            hidden[b, tile_rows(i), :] = (0.5 * u * (1.0 + tangent)).astype(bf16)
            slope[b, tile_rows(i), :] = 0.5 * (1.0 + tangent) + 0.5 * u * (1.0 - tangent * tangent) * gelu_scale * (
                1.0 + 3.0 * gelu_cubic * u * u
            )

    nt = (((1,), (1,)), ((), ()))
    split = features // 2

    def project(r, h):
        value = 0.0
        for b in range(2):
            value = value + lax.dot_general(
                hidden[b, half(r), :],
                second[b, pl.ds(pl.multiple_of(h * split, 128), split), :],
                nt,
                preferred_element_type=f32,
            )
        return value

    near = q // 2
    for step, h in enumerate((near, 1 - near)):
        if step == 0:
            for b, slot in ((0, 3), (1, 3), (0, 5), (1, 6)):
                from_mate(1, b, slot)
        else:
            got(1, 0, 4)
            got(1, 1, 4)
            for b, slot in ((0, 6), (1, 5), (0, 7), (1, 7)):
                from_mate(1, b, slot)
        part_out[h] = project(1, h).astype(bf16)
        send(part_out.at[h], part_in.at[h], ps.at[step], pr.at[step], pair)
    for h in range(2):
        unit[:, pl.ds(h * split, split)] = project(0, h)

    for k in range(1, replicas):
        origin = (d + replicas - k) % replicas
        arrive(
            coming.at[pl.ds(pl.multiple_of(origin * slot_rows, slot_rows), slot_rows)], ur.at[k], us.at[k]
        )
    picker = jnp.where(slot_col == lanes, 1.0, 0.0).astype(bf16)
    cot[...] = jnp.dot(picker, coming[...], preferred_element_type=f32)
    for step, h in enumerate((near, 1 - near)):
        arrive(part_in.at[h], pr.at[step], ps.at[step])

    def norm_tile(i):
        rows = tile_rows(i)
        partner = jnp.concatenate([part_in[h, rows, :].astype(f32) for h in range(2)], axis=1)
        residual = rows_in[rows, :].astype(f32) + (unit[rows, :] + partner)
        unit_out, scale_out = normalize(residual)
        merged[rows, :] = (unit_out * merge_gain[...][None, :] + merge_bias[...][None, :]).astype(bf16)
        grad_rows[rows, :] = norm_backward(cot[rows, :], unit_out, scale_out, merge_gain[...][None, :]).astype(bf16)

    tiles = share // TILE // 2
    for step in range(2):
        pl.loop(step * tiles, (step + 1) * tiles)(norm_tile)
        send(
            grad_rows.at[pl.ds(step * tiles * TILE, tiles * TILE)],
            grad_rows.at[pl.ds(share + step * tiles * TILE, tiles * TILE)],
            xs.at[step],
            xr.at[step],
            pair,
        )

    picker_t = jnp.where(subs == slot_row, 1.0, 0.0).astype(bf16)
    outgoing[...] = jnp.dot(picker_t, merged[...], preferred_element_type=f32).astype(bf16)
    own_slots = pl.ds(pl.multiple_of(d * slot_rows, slot_rows), slot_rows)
    keep = pltpu.make_async_copy(outgoing.at[own_slots], received.at[own_slots], local_sem.at[5])
    keep.start()
    for k in range(1, replicas):
        peer = (d + k) % replicas
        send(
            outgoing.at[pl.ds(pl.multiple_of(peer * slot_rows, slot_rows), slot_rows)],
            received.at[own_slots],
            os_.at[k],
            or_.at[k],
            (s, peer),
        )

    def back(r):
        for b in range(2):
            grad_hidden = jnp.dot(grad_rows[half(r), :], second[b], preferred_element_type=f32)
            grad_pre[b, half(r), :] = (grad_hidden * slope[b, half(r), :]).astype(bf16)

    flip(grad_rows, grad_rows_t, 0)
    back(0)
    for step in range(2):
        arrive(
            grad_rows.at[pl.ds(share + step * tiles * TILE, tiles * TILE)], xr.at[step], xs.at[step]
        )
    flip(grad_rows, grad_rows_t, 1)

    def piece(w, j, b):
        lhs, rhs = ((normed_t, grad_pre), (grad_rows_t, hidden))[w]
        return jnp.dot(lhs[shard_rows(j), :], rhs[b], preferred_element_type=f32)

    def both_cores(w, b, k, chip):
        value = piece(w, chip * 2 + c, b)
        arrive(core_in.at[w, b, k], cr.at[w, b, k], cs.at[w, b, k])
        return value + core_in[w, b, k].astype(f32)

    def pass_on(w, b, k, value, chip):
        chip_out[w, b, k] = value.astype(bf16)
        send(chip_out.at[w, b, k], chip_in.at[w, b, k], hs.at[w, b, k], hr.at[w, b, k], (s, chip * 2 + c))

    def taken(w, b, k):
        arrive(chip_in.at[w, b, k], hr.at[w, b, k], hs.at[w, b, k])
        return chip_in[w, b, k].astype(f32)

    def to_core(w, b, chosen):
        for k in chosen:
            chip = (corner, *side(w, b), q)[k]
            core_out[w, b, k] = piece(w, chip * 2 + mate_core, b).astype(bf16)
            send(core_out.at[w, b, k], core_in.at[w, b, k], cs.at[w, b, k], cr.at[w, b, k], mate)

    def begin(w, b):
        lead = side(w, b)[0]
        to_core(w, b, (0, 1))
        pass_on(w, b, 0, both_cores(w, b, 0, corner), lead)
        pass_on(w, b, 1, both_cores(w, b, 1, lead), lead)

    def middle(w, b):
        follow = side(w, b)[1]
        to_core(w, b, (2, 3))
        value = both_cores(w, b, 2, follow)
        pass_on(w, b, 2, value + taken(w, b, 0), follow)
        total[w, b] = both_cores(w, b, 3, q)

    def close(w, b):
        value = total[w, b] + taken(w, b, 1)
        value = value + taken(w, b, 2)
        if b:
            cross_out[w] = value.astype(bf16)
            send(cross_out.at[w], cross_in.at[w], zs.at[w], zr.at[w], across)
        else:
            total[w, 0] = value

    def finish(w, out):
        arrive(cross_in.at[w], zr.at[w], zs.at[w])
        out[...] = total[w, 0] + cross_in[w].astype(f32)

    begin(1, 1)
    back(1)
    begin(0, 1)
    middle(1, 1)
    begin(1, 0)
    middle(0, 1)
    begin(0, 0)
    close(1, 1)
    middle(1, 0)
    close(0, 1)
    middle(0, 0)
    keep.wait()
    for k in range(1, replicas):
        origin = (d + replicas - k) % replicas
        arrive(
            received.at[pl.ds(pl.multiple_of(origin * slot_rows, slot_rows), slot_rows)], or_.at[k], os_.at[k]
        )
    close(1, 0)
    finish(1, grad_out)
    close(0, 0)
    finish(0, grad_in)
    for copy in sent:
        copy.wait_send()


def in_one_kernel(patches, pre_gain, merge_gain, merge_bias, w_in, w_out, destinations, upstream):
    sections = lax.axis_size("section")
    replicas = lax.axis_size("dp")
    chips = replicas // 2
    share = patches.shape[0] // sections
    features = patches.shape[1]
    merge = upstream.shape[1] // features
    blocks, width = destinations.shape[0], w_in.shape[1]
    shard = w_in.shape[0]
    capacity = upstream.shape[0] // replicas
    f32, bf16 = jnp.float32, jnp.bfloat16
    targets = jnp.repeat(destinations[:, 0], merge).astype(f32)
    block_ids = np.repeat(np.arange(blocks), merge).astype(np.float32)
    member = np.tile(np.arange(merge), blocks).astype(np.float32)
    vmem = pl.BlockSpec(memory_space=pltpu.VMEM)
    hbm = pl.BlockSpec(memory_space=pl.ANY)
    dma = pltpu.SemaphoreType.DMA
    received, grad_in, grad_out_t = pl.pallas_call(
        functools.partial(window_kernel, sections, replicas, merge, capacity),
        out_shape=(
            jax.ShapeDtypeStruct((upstream.shape[0] * merge, features), bf16),
            jax.ShapeDtypeStruct((shard, width), f32),
            jax.ShapeDtypeStruct((shard, width), f32),
        ),
        in_specs=[hbm, vmem, vmem, vmem, hbm, hbm] + [vmem] * 6 + [hbm],
        out_specs=(hbm, vmem, vmem),
        scratch_shapes=[
            pltpu.VMEM((2 * share, features), bf16),
            pltpu.VMEM((2 * share, features), bf16),
            pltpu.VMEM((features, 2 * share), bf16),
            pltpu.VMEM((2, features, width), bf16),
            pltpu.VMEM((2, features, width), bf16),
            pltpu.VMEM((2, 2 * share, width), f32),
            pltpu.VMEM((2, 2 * share, width), bf16),
            pltpu.VMEM((2, share, features // 2), bf16),
            pltpu.VMEM((2, share, features // 2), bf16),
            pltpu.VMEM((share, features), f32),
            pltpu.VMEM((8, 128), f32),
            pltpu.VMEM((share, features), bf16),
            pltpu.VMEM((share, features), bf16),
            pltpu.VMEM((share, features), bf16),
            pltpu.VMEM((share, features), f32),
            pltpu.VMEM((2 * share, features), bf16),
            pltpu.VMEM((features, 2 * share), bf16),
            pltpu.VMEM((2, 2 * share, width), bf16),
            pltpu.VMEM((2, 2, chips, shard, width), bf16),
            pltpu.VMEM((2, 2, chips, shard, width), bf16),
            pltpu.VMEM((2, 2, chips - 1, shard, width), bf16),
            pltpu.VMEM((2, 2, chips - 1, shard, width), bf16),
            pltpu.VMEM((2, 2, shard, width), f32),
            pltpu.VMEM((2, shard, width), bf16),
            pltpu.VMEM((2, shard, width), bf16),
            dma((6,)),
            dma((2, 2, 2 * chips)),
            dma((2, 2, 2 * chips)),
            dma((replicas,)),
            dma((replicas,)),
            dma((replicas,)),
            dma((replicas,)),
            dma((2,)),
            dma((2,)),
            dma((2,)),
            dma((2,)),
            dma((2, 2, chips)),
            dma((2, 2, chips)),
            dma((2, 2, chips - 1)),
            dma((2, 2, chips - 1)),
            dma((2,)),
            dma((2,)),
        ],
        compiler_params=pltpu.CompilerParams(
            collective_id=0, has_side_effects=True, vmem_limit_bytes=60 * 1024 * 1024
        ),
    )(
        patches,
        pre_gain,
        merge_gain,
        merge_bias,
        w_in,
        w_out.T,
        targets[:, None],
        targets[None, :],
        block_ids[:, None],
        block_ids[None, :],
        member[:, None],
        member[None, :],
        upstream.reshape(-1, features),
    )
    return (received.reshape(upstream.shape), grad_in, grad_out_t.T)


def window(*args):
    patches, w_in, upstream = args[0], args[4], args[7]
    sections = lax.axis_size("section")
    replicas = lax.axis_size("dp")
    share = patches.shape[0] // sections
    slots = upstream.shape[0] * upstream.shape[1] // patches.shape[1]
    aligned = w_in.shape[0] % 16 == 0 and w_in.shape[1] % 128 == 0 and patches.shape[1] % 256 == 0
    if aligned and sections == 4 and replicas == 8 and slots == share:
        return in_one_kernel(*args)
    return on_device(*args)


def solution(mesh):
    return jax.shard_map(
        window,
        mesh=mesh,
        in_specs=(
            P("dp", None),
            P(),
            P(),
            P(),
            P("dp", "section"),
            P("section", "dp"),
            P(("section", "dp"), None),
            P(("section", "dp"), None),
        ),
        out_specs=(P(("section", "dp"), None), P("dp", "section"), P("section", "dp")),
        check_vma=False,
    )
```

```python
import functools

import jax
import jax.numpy as jnp
import numpy as np
from jax import lax
from jax.experimental import pallas as pl
from jax.experimental.pallas import tpu as pltpu
from jax.sharding import PartitionSpec as P

BLK = 1


epsilon = 1e-06
gelu_scale = 0.7978845608028654
gelu_cubic = 0.044715


def gelu_slope(values):
    tangent = jnp.tanh(gelu_scale * (values + gelu_cubic * values * values * values))
    return 0.5 * (1.0 + tangent) + 0.5 * values * (1.0 - tangent * tangent) * gelu_scale * (
        1.0 + 3.0 * gelu_cubic * values * values
    )


def normalize(values):
    average = jnp.mean(values, axis=-1, keepdims=True)
    centred = values - average
    inv_scale = lax.rsqrt(jnp.mean(centred * centred, axis=-1, keepdims=True) + epsilon)
    return (centred * inv_scale, inv_scale)


def norm_backward(cotangent, unit_rows, inv_scale, gain):
    scaled = cotangent * gain
    return inv_scale * (
        scaled
        - jnp.mean(scaled, axis=-1, keepdims=True)
        - unit_rows * jnp.mean(scaled * unit_rows, axis=-1, keepdims=True)
    )


def block_ranks(targets):
    block_count = targets.shape[-1]
    matches = targets[:, None] == targets[None, :]
    earlier = lax.broadcasted_iota(jnp.int32, (block_count, block_count), 1) < lax.broadcasted_iota(
        jnp.int32, (block_count, block_count), 0
    )
    return jnp.sum((matches & earlier).astype(jnp.int32), axis=-1)


def on_device(patches, pre_gain, merge_gain, merge_bias, w_in, w_out, destinations, upstream):
    sections = lax.axis_size("section")
    replicas = lax.axis_size("dp")
    group_rows = patches.shape[0]
    share_rows = group_rows // sections
    feature_count = patches.shape[1]
    merged_width = upstream.shape[1]
    block_width = BLK * merged_width
    block_count = destinations.shape[0]
    capacity = upstream.shape[0] // (replicas * BLK)
    inputs = patches.astype(jnp.float32)
    unit_rows, _ = normalize(inputs)
    normed = (unit_rows * pre_gain).astype(jnp.bfloat16)
    preact = jnp.dot(
        normed, lax.all_gather(w_in, "dp", axis=0, tiled=True), preferred_element_type=jnp.float32
    )
    hidden = jax.nn.gelu(preact, approximate=True).astype(jnp.bfloat16)
    out_full = lax.all_gather(w_out, "dp", axis=1, tiled=True)
    partial_value = jnp.dot(hidden, out_full, preferred_element_type=jnp.float32).astype(jnp.bfloat16)
    row_start = lax.axis_index("section") * share_rows
    own_inputs = lax.dynamic_slice_in_dim(inputs, row_start, share_rows, 0)
    residual = own_inputs + lax.psum_scatter(
        partial_value, "section", scatter_dimension=0, tiled=True
    ).astype(jnp.float32)
    unit_out, scale_out = normalize(residual)
    merged = (unit_out * merge_gain + merge_bias).astype(jnp.bfloat16)
    blocks = merged.reshape(block_count, block_width)
    targets = destinations[:, 0]
    block_rank = block_ranks(targets)
    column_ids = lax.broadcasted_iota(jnp.int32, (block_count, replicas * capacity), 1)
    picker = ((targets * capacity + block_rank)[:, None] == column_ids).astype(jnp.bfloat16)
    outgoing = lax.dot_general(
        picker, blocks, (((0,), (0,)), ((), ())), preferred_element_type=jnp.float32
    ).astype(jnp.bfloat16)
    arrived = lax.all_to_all(
        outgoing.reshape(replicas, capacity * block_width),
        "dp",
        split_axis=0,
        concat_axis=0,
        tiled=True,
    )
    received = arrived.reshape(replicas * capacity * BLK, merged_width)
    coming = lax.all_to_all(
        upstream.reshape(replicas, capacity * block_width),
        "dp",
        split_axis=0,
        concat_axis=0,
        tiled=True,
    )
    cotangent = jnp.dot(
        picker, coming.reshape(replicas * capacity, block_width), preferred_element_type=jnp.float32
    )
    cotangent = cotangent.astype(jnp.bfloat16).reshape(share_rows, feature_count)
    grad_own = norm_backward(cotangent.astype(jnp.float32), unit_out, scale_out, merge_gain).astype(
        jnp.bfloat16
    )
    grad_residual = lax.all_gather(grad_own, "section", axis=0, tiled=True)
    grad_second = lax.dot_general(
        hidden, grad_residual, (((0,), (0,)), ((), ())), preferred_element_type=jnp.float32
    )
    grad_hidden = lax.dot_general(
        grad_residual, out_full, (((1,), (1,)), ((), ())), preferred_element_type=jnp.float32
    )
    grad_preact = (grad_hidden * gelu_slope(preact)).astype(jnp.bfloat16)
    grad_first = lax.dot_general(
        normed, grad_preact, (((0,), (0,)), ((), ())), preferred_element_type=jnp.float32
    )
    grad_w_in, grad_w_out = (
        lax.psum_scatter(grad_first.astype(jnp.bfloat16), "dp", scatter_dimension=0, tiled=True).astype(jnp.float32),
        lax.psum_scatter(grad_second.astype(jnp.bfloat16), "dp", scatter_dimension=1, tiled=True).astype(jnp.float32),
    )
    return (received, grad_w_in, grad_w_out)


TILE = 32


def remote(src, dst, send_sem, recv_sem, device):
    return pltpu.make_async_remote_copy(
        src_ref=src,
        dst_ref=dst,
        send_sem=send_sem,
        recv_sem=recv_sem,
        device_id=device,
        device_id_type=pl.DeviceIdType.MESH,
    )


def window_kernel(
    sections, replicas, merge, capacity,
    patches, pre_gain, merge_gain, merge_bias, w_in, w_out_t, tcol, trow, bcol, brow, mcol, mrow, upstream,
    received, grad_in, grad_out,
    rows_in, normed, normed_t, first, second, slope, hidden, part_out, part_in, unit, inv, merged, outgoing,
    coming, cot, grad_rows, grad_rows_t, grad_pre, core_out, core_in, chip_out, chip_in, total, cross_out,
    cross_in, local_sem, gs, gr, us, ur, os_, or_, ps, pr, xs, xr, cs, cr, hs, hr, zs, zr,
):
    share = rows_in.shape[0] // 2
    features = rows_in.shape[1]
    width = w_in.shape[1]
    shard = w_in.shape[0]
    chips = replicas // 2
    f32, bf16 = jnp.float32, jnp.bfloat16
    s, d = lax.axis_index("section"), lax.axis_index("dp")
    q, c = d // 2, d % 2
    pair = (s + 1 - 2 * (s % 2), d)
    across = ((s + sections // 2) % sections, d)
    mate_core = 1 - c
    mate = (s, q * 2 + mate_core)

    beside, below = q + 1 - 2 * (q % 2), (q + 2) % chips
    corner = (beside + 2) % chips

    def side(w, b):
        return (below, beside) if w == b else (beside, below)

    def shard_rows(j):
        return pl.ds(pl.multiple_of(j * shard, 16), shard)

    sent = []

    def send(*args):
        copy = remote(*args)
        copy.start()
        sent.append(copy)

    def arrive(dst, recv_sem, send_sem):
        remote(dst, dst, send_sem, recv_sem, mate).wait_recv()

    shards, fulls = (w_in, w_out_t), (first, second)
    loads = [
        pltpu.make_async_copy(
            patches.at[pl.ds(pl.multiple_of(s * share, share), share)], rows_in.at[pl.ds(0, share)], local_sem.at[0]
        ),
        pltpu.make_async_copy(
            patches.at[pl.ds(pl.multiple_of(pair[0] * share, share), share)],
            rows_in.at[pl.ds(share, share)],
            local_sem.at[1],
        ),
        pltpu.make_async_copy(w_in, first.at[0, shard_rows(d)], local_sem.at[2]),
        pltpu.make_async_copy(w_out_t, second.at[0, shard_rows(d)], local_sem.at[3]),
    ]
    slots = replicas * capacity
    loads.append(
        pltpu.make_async_copy(
            upstream.at[d],
            coming.at[d],
            local_sem.at[4],
        )
    )
    for copy in loads:
        copy.start()

    barrier = pltpu.get_barrier_semaphore()
    for k in range(1, replicas):
        pl.semaphore_signal(
            barrier, inc=1, device_id=(s, (d + k) % replicas), device_id_type=pl.DeviceIdType.MESH
        )
    for peer in (pair, across):
        pl.semaphore_signal(barrier, inc=1, device_id=peer, device_id_type=pl.DeviceIdType.MESH)
    pl.semaphore_wait(barrier, replicas + 1)

    for w in range(2):
        send(shards[w], fulls[w].at[1, shard_rows(d)], gs.at[w, 1, 0], gr.at[w, 1, 0], across)

    def spread(w, b):
        src = shards[w] if b == 0 else fulls[w].at[1, shard_rows(d)]
        place = fulls[w].at[b, shard_rows(d)]
        peers = [(s, chip * 2 + c) for chip in side(w, b)] + [mate]
        for slot, peer in enumerate(peers, 1):
            send(src, place, gs.at[w, b, slot], gr.at[w, b, slot], peer)

    def origin_of(w, b, slot):
        return {1: side(w, b)[0], 2: side(w, b)[1], 4: corner}[slot]

    def got(w, b, slot):
        place = fulls[w].at[b, shard_rows(origin_of(w, b, slot) * 2 + c)]
        arrive(place, gr.at[w, b, slot], gs.at[w, b, slot])
        if slot == 1:
            send(place, place, gs.at[w, b, 4], gr.at[w, b, 4], (s, side(w, b)[1] * 2 + c))
        to_mate = {1: 5, 2: 6, 4: 7}[slot]
        send(place, place, gs.at[w, b, to_mate], gr.at[w, b, to_mate], mate)

    def from_mate(w, b, slot):
        chip = q if slot == 3 else origin_of(w, b, {5: 1, 6: 2, 7: 4}[slot])
        arrive(fulls[w].at[b, shard_rows(chip * 2 + mate_core)], gr.at[w, b, slot], gs.at[w, b, slot])

    spread(0, 0)
    spread(1, 0)
    got(0, 0, 1)
    got(1, 0, 1)
    arrive(first.at[1, shard_rows(d)], gr.at[0, 1, 0], gs.at[0, 1, 0])
    spread(0, 1)
    arrive(second.at[1, shard_rows(d)], gr.at[1, 1, 0], gs.at[1, 1, 0])
    spread(1, 1)

    for copy in loads:
        copy.wait()

    def tile_rows(i):
        return pl.ds(pl.multiple_of(i * TILE, TILE), TILE)

    @pl.loop(0, 2 * share // TILE)
    def _(i):
        unit_rows, _ = normalize(rows_in[tile_rows(i), :].astype(f32))
        normed[tile_rows(i), :] = (unit_rows * pre_gain[...][None, :]).astype(bf16)

    def flip(src, dst, r):
        @pl.loop(0, features // 128)
        def _(i):
            cols = pl.ds(pl.multiple_of(i * 128, 128), 128)
            dst[cols, pl.ds(r * share, share)] = src[pl.ds(r * share, share), cols].T

    got(0, 0, 2)
    got(0, 0, 4)
    got(0, 1, 1)
    got(1, 1, 1)
    flip(normed, normed_t, 0)
    flip(normed, normed_t, 1)
    for k in range(1, replicas):
        peer = (d + k) % replicas
        send(
            upstream.at[peer],
            coming.at[d],
            us.at[k],
            ur.at[k],
            (s, peer),
        )

    matches = tcol[...] == trow[...]
    above = jnp.where(matches & (brow[...] < bcol[...]) & (mrow[...] == 0.0), 1.0, 0.0)
    left = jnp.where(matches & (bcol[...] < brow[...]) & (mcol[...] == 0.0), 1.0, 0.0)
    slot_col = (tcol[...] * capacity + jnp.sum(above, axis=1, keepdims=True)) * merge + mcol[...]
    slot_row = (trow[...] * capacity + jnp.sum(left, axis=0, keepdims=True)) * merge + mrow[...]
    lanes = lax.broadcasted_iota(jnp.int32, (share, slots), 1).astype(f32) * merge
    subs = lax.broadcasted_iota(jnp.int32, (slots, share), 0).astype(f32) * merge

    def half(r):
        return pl.ds(r * share, share)

    for b in range(2):
        if b == 1:
            got(0, 1, 2)
            got(0, 1, 4)
        for slot in (3, 5, 6, 7):
            from_mate(0, b, slot)
        for r in range(2):
            slope[b, half(r), :] = jnp.dot(normed[half(r), :], first[b], preferred_element_type=f32)
        if b == 0:
            got(1, 0, 2)
            got(1, 1, 2)

        @pl.loop(0, 2 * share // TILE)
        def _(i):
            u = slope[b, tile_rows(i), :]
            tangent = jnp.tanh(gelu_scale * (u + gelu_cubic * u * u * u))
            hidden[b, tile_rows(i), :] = (0.5 * u * (1.0 + tangent)).astype(bf16)
            slope[b, tile_rows(i), :] = 0.5 * (1.0 + tangent) + 0.5 * u * (1.0 - tangent * tangent) * gelu_scale * (
                1.0 + 3.0 * gelu_cubic * u * u
            )

    nt = (((1,), (1,)), ((), ()))
    split = features // 2

    def project(r, h):
        value = 0.0
        for b in range(2):
            value = value + lax.dot_general(
                hidden[b, half(r), :],
                second[b, pl.ds(pl.multiple_of(h * split, 128), split), :],
                nt,
                preferred_element_type=f32,
            )
        return value

    near = q // 2
    for step, h in enumerate((near, 1 - near)):
        if step == 0:
            for b, slot in ((0, 3), (1, 3), (0, 5), (1, 6)):
                from_mate(1, b, slot)
        else:
            got(1, 0, 4)
            got(1, 1, 4)
            for b, slot in ((0, 6), (1, 5), (0, 7), (1, 7)):
                from_mate(1, b, slot)
        part_out[h] = project(1, h).astype(bf16)
        send(part_out.at[h], part_in.at[h], ps.at[step], pr.at[step], pair)
    for h in range(2):
        unit[:, pl.ds(h * split, split)] = project(0, h)

    for k in range(1, replicas):
        origin = (d + replicas - k) % replicas
        arrive(
            coming.at[origin], ur.at[k], us.at[k]
        )
    value = 0.0
    for m in range(merge):
        picker = jnp.where(slot_col == lanes + m, 1.0, 0.0).astype(bf16)
        part = coming[:, :, pl.ds(m * features, features)].astype(f32).reshape(slots, features)
        value = value + jnp.dot(picker, part.astype(bf16), preferred_element_type=f32)
    cot[...] = value
    for step, h in enumerate((near, 1 - near)):
        arrive(part_in.at[h], pr.at[step], ps.at[step])

    def norm_tile(i):
        rows = tile_rows(i)
        partner = jnp.concatenate([part_in[h, rows, :].astype(f32) for h in range(2)], axis=1)
        residual = rows_in[rows, :].astype(f32) + (unit[rows, :] + partner)
        unit_out, scale_out = normalize(residual)
        merged[rows, :] = (unit_out * merge_gain[...][None, :] + merge_bias[...][None, :]).astype(bf16)
        grad_rows[rows, :] = norm_backward(cot[rows, :], unit_out, scale_out, merge_gain[...][None, :]).astype(bf16)

    tiles = share // TILE // 2
    for step in range(2):
        pl.loop(step * tiles, (step + 1) * tiles)(norm_tile)
        send(
            grad_rows.at[pl.ds(step * tiles * TILE, tiles * TILE)],
            grad_rows.at[pl.ds(share + step * tiles * TILE, tiles * TILE)],
            xs.at[step],
            xr.at[step],
            pair,
        )

    for m in range(merge):
        picker_t = jnp.where(subs + m == slot_row, 1.0, 0.0).astype(bf16)
        part = jnp.dot(picker_t, merged[...], preferred_element_type=f32)
        outgoing[:, :, pl.ds(m * features, features)] = part.reshape(replicas, capacity, features).astype(bf16)
    keep = pltpu.make_async_copy(outgoing.at[d], received.at[d], local_sem.at[5])
    keep.start()
    for k in range(1, replicas):
        peer = (d + k) % replicas
        send(
            outgoing.at[peer],
            received.at[d],
            os_.at[k],
            or_.at[k],
            (s, peer),
        )

    def back(r):
        for b in range(2):
            grad_hidden = jnp.dot(grad_rows[half(r), :], second[b], preferred_element_type=f32)
            grad_pre[b, half(r), :] = (grad_hidden * slope[b, half(r), :]).astype(bf16)

    flip(grad_rows, grad_rows_t, 0)
    back(0)
    for step in range(2):
        arrive(
            grad_rows.at[pl.ds(share + step * tiles * TILE, tiles * TILE)], xr.at[step], xs.at[step]
        )
    flip(grad_rows, grad_rows_t, 1)

    def piece(w, j, b):
        lhs, rhs = ((normed_t, grad_pre), (grad_rows_t, hidden))[w]
        return jnp.dot(lhs[shard_rows(j), :], rhs[b], preferred_element_type=f32)

    def both_cores(w, b, k, chip):
        value = piece(w, chip * 2 + c, b)
        arrive(core_in.at[w, b, k], cr.at[w, b, k], cs.at[w, b, k])
        return value + core_in[w, b, k].astype(f32)

    def pass_on(w, b, k, value, chip):
        chip_out[w, b, k] = value.astype(bf16)
        send(chip_out.at[w, b, k], chip_in.at[w, b, k], hs.at[w, b, k], hr.at[w, b, k], (s, chip * 2 + c))

    def taken(w, b, k):
        arrive(chip_in.at[w, b, k], hr.at[w, b, k], hs.at[w, b, k])
        return chip_in[w, b, k].astype(f32)

    def to_core(w, b, chosen):
        for k in chosen:
            chip = (corner, *side(w, b), q)[k]
            core_out[w, b, k] = piece(w, chip * 2 + mate_core, b).astype(bf16)
            send(core_out.at[w, b, k], core_in.at[w, b, k], cs.at[w, b, k], cr.at[w, b, k], mate)

    def begin(w, b):
        lead = side(w, b)[0]
        to_core(w, b, (0, 1))
        pass_on(w, b, 0, both_cores(w, b, 0, corner), lead)
        pass_on(w, b, 1, both_cores(w, b, 1, lead), lead)

    def middle(w, b):
        follow = side(w, b)[1]
        to_core(w, b, (2, 3))
        value = both_cores(w, b, 2, follow)
        pass_on(w, b, 2, value + taken(w, b, 0), follow)
        total[w, b] = both_cores(w, b, 3, q)

    def close(w, b):
        value = total[w, b] + taken(w, b, 1)
        value = value + taken(w, b, 2)
        if b:
            cross_out[w] = value.astype(bf16)
            send(cross_out.at[w], cross_in.at[w], zs.at[w], zr.at[w], across)
        else:
            total[w, 0] = value

    def finish(w, out):
        arrive(cross_in.at[w], zr.at[w], zs.at[w])
        out[...] = total[w, 0] + cross_in[w].astype(f32)

    begin(1, 1)
    back(1)
    begin(0, 1)
    middle(1, 1)
    begin(1, 0)
    middle(0, 1)
    begin(0, 0)
    close(1, 1)
    middle(1, 0)
    close(0, 1)
    middle(0, 0)
    keep.wait()
    for k in range(1, replicas):
        origin = (d + replicas - k) % replicas
        arrive(
            received.at[origin], or_.at[k], os_.at[k]
        )
    close(1, 0)
    finish(1, grad_out)
    close(0, 0)
    finish(0, grad_in)
    for copy in sent:
        copy.wait_send()


def in_one_kernel(patches, pre_gain, merge_gain, merge_bias, w_in, w_out, destinations, upstream):
    sections = lax.axis_size("section")
    replicas = lax.axis_size("dp")
    chips = replicas // 2
    share = patches.shape[0] // sections
    features = patches.shape[1]
    merge = upstream.shape[1] // features
    blocks, width = destinations.shape[0], w_in.shape[1]
    shard = w_in.shape[0]
    capacity = upstream.shape[0] // replicas
    f32, bf16 = jnp.float32, jnp.bfloat16
    targets = jnp.repeat(destinations[:, 0], merge).astype(f32)
    block_ids = np.repeat(np.arange(blocks), merge).astype(np.float32)
    member = np.tile(np.arange(merge), blocks).astype(np.float32)
    vmem = pl.BlockSpec(memory_space=pltpu.VMEM)
    hbm = pl.BlockSpec(memory_space=pl.ANY)
    dma = pltpu.SemaphoreType.DMA
    received, grad_in, grad_out_t = pl.pallas_call(
        functools.partial(window_kernel, sections, replicas, merge, capacity),
        out_shape=(
            jax.ShapeDtypeStruct((replicas, capacity, upstream.shape[1]), bf16),
            jax.ShapeDtypeStruct((shard, width), f32),
            jax.ShapeDtypeStruct((shard, width), f32),
        ),
        in_specs=[hbm, vmem, vmem, vmem, hbm, hbm] + [vmem] * 6 + [hbm],
        out_specs=(hbm, vmem, vmem),
        scratch_shapes=[
            pltpu.VMEM((2 * share, features), bf16),
            pltpu.VMEM((2 * share, features), bf16),
            pltpu.VMEM((features, 2 * share), bf16),
            pltpu.VMEM((2, features, width), bf16),
            pltpu.VMEM((2, features, width), bf16),
            pltpu.VMEM((2, 2 * share, width), f32),
            pltpu.VMEM((2, 2 * share, width), bf16),
            pltpu.VMEM((2, share, features // 2), bf16),
            pltpu.VMEM((2, share, features // 2), bf16),
            pltpu.VMEM((share, features), f32),
            pltpu.VMEM((8, 128), f32),
            pltpu.VMEM((share, features), bf16),
            pltpu.VMEM((replicas, capacity, upstream.shape[1]), bf16),
            pltpu.VMEM((replicas, capacity, upstream.shape[1]), bf16),
            pltpu.VMEM((share, features), f32),
            pltpu.VMEM((2 * share, features), bf16),
            pltpu.VMEM((features, 2 * share), bf16),
            pltpu.VMEM((2, 2 * share, width), bf16),
            pltpu.VMEM((2, 2, chips, shard, width), bf16),
            pltpu.VMEM((2, 2, chips, shard, width), bf16),
            pltpu.VMEM((2, 2, chips - 1, shard, width), bf16),
            pltpu.VMEM((2, 2, chips - 1, shard, width), bf16),
            pltpu.VMEM((2, 2, shard, width), f32),
            pltpu.VMEM((2, shard, width), bf16),
            pltpu.VMEM((2, shard, width), bf16),
            dma((6,)),
            dma((2, 2, 2 * chips)),
            dma((2, 2, 2 * chips)),
            dma((replicas,)),
            dma((replicas,)),
            dma((replicas,)),
            dma((replicas,)),
            dma((2,)),
            dma((2,)),
            dma((2,)),
            dma((2,)),
            dma((2, 2, chips)),
            dma((2, 2, chips)),
            dma((2, 2, chips - 1)),
            dma((2, 2, chips - 1)),
            dma((2,)),
            dma((2,)),
        ],
        compiler_params=pltpu.CompilerParams(
            collective_id=0, has_side_effects=True, vmem_limit_bytes=60 * 1024 * 1024
        ),
    )(
        patches,
        pre_gain,
        merge_gain,
        merge_bias,
        w_in,
        w_out.T,
        targets[:, None],
        targets[None, :],
        block_ids[:, None],
        block_ids[None, :],
        member[:, None],
        member[None, :],
        upstream.reshape(replicas, capacity, -1),
    )
    return (received.reshape(upstream.shape), grad_in, grad_out_t.T)


def window(*args):
    patches, w_in, upstream = args[0], args[4], args[7]
    sections = lax.axis_size("section")
    replicas = lax.axis_size("dp")
    share = patches.shape[0] // sections
    slots = upstream.shape[0] * upstream.shape[1] // patches.shape[1]
    aligned = w_in.shape[0] % 16 == 0 and w_in.shape[1] % 128 == 0 and patches.shape[1] % 256 == 0
    if aligned and sections == 4 and replicas == 8 and slots == share:
        return in_one_kernel(*args)
    return on_device(*args)


def solution(mesh):
    return jax.shard_map(
        window,
        mesh=mesh,
        in_specs=(
            P("dp", None),
            P(),
            P(),
            P(),
            P("dp", "section"),
            P("section", "dp"),
            P(("section", "dp"), None),
            P(("section", "dp"), None),
        ),
        out_specs=(P(("section", "dp"), None), P("dp", "section"), P("section", "dp")),
        check_vma=False,
    )
```
